32 devices in a mesh: ty: 4 (over y, core), tx: 8 (over z, x).
Axes of the slice: x: 2, y: 2, z: 4, core: 2. Of those that a mesh axis runs over, the one named last changes fastest.
Arguments:
- object_field: bfloat16 [2, 1024, 2048], P(None, 'ty', 'tx'), may hold values from -5 to 5
- probe_field: float32 [2, 256, 256], replicated, may hold values from -2.1 to 2.1
- corners: int32 [4, 8, 8, 2], P('ty', 'tx'), may hold values from 0 to 255, as said below
- counts: int32 [4, 8], P('ty', 'tx'), may hold values from 0 to 8, as said below
- intensity: bfloat16 [4, 8, 8, 256, 256], P('ty', 'tx'), may hold values from 0 to 1.5
- damping: float32 [], replicated, may hold values from 0.5 to 4
Outputs:
- update: float32 [2, 1024, 2048], P(None, 'ty', 'tx')
The draws below stay inside these ranges and needn't reach their ends.
Inputs may be any that keep to these rules, and one draw needn't show every extreme that they name: `corners`: A patch lies inside the object: on the last tile row (column) of devices the corner's row (column) is 0. A device's live slots are its first counts slots. The counts of the devices of one column (same tx index) sum to exactly 16, and some device of every column holds 8.
All inputs are finite; a program needn't handle non-finite values.
Results may differ from the reference program's by a relative error of at most 0.015.
Values may be sent and summed in bfloat16 or wider, within the bound.
A program may use at most 64 MiB of HBM per device.

```python
import math
import jax
import jax.numpy as jnp
from jax import lax

W = 256
TILE = 256
ITERS = 2
SLOTS = 8
ROW_TILES = 4
COL_TILES = 8
NROW = 1024
NCOL = 2048
POSITIONS = 128


def draw_object_field(key, part):
    amp_key, phase_key = jax.random.split(key)
    row_frac = jnp.arange(NROW, dtype=jnp.float32)[:, None] / NROW
    col_frac = jnp.arange(NCOL, dtype=jnp.float32)[None, :] / NCOL
    slope_ramp = jnp.exp(0.5 * math.log(3.0) * (row_frac + col_frac))
    roughness = jnp.exp(jax.random.uniform(amp_key, (NROW, NCOL), jnp.float32, math.log(0.5), math.log(1.5)))
    phases = jax.random.uniform(phase_key, (NROW, NCOL), jnp.float32, -math.pi, math.pi)
    amplitude = slope_ramp * roughness
    return jnp.stack([amplitude * jnp.cos(phases), amplitude * jnp.sin(phases)], 0).astype(jnp.bfloat16)


def draw_corners(key, part):
    drawn = jax.random.randint(key, (ROW_TILES, COL_TILES, SLOTS, 2), 0, TILE)
    last_row = jnp.arange(ROW_TILES, dtype=jnp.int32)[:, None, None] == ROW_TILES - 1
    last_col = jnp.arange(COL_TILES, dtype=jnp.int32)[None, :, None] == COL_TILES - 1
    row_corner = jnp.where(last_row, jnp.minimum(drawn[..., 0], TILE - W), drawn[..., 0])
    col_corner = jnp.where(last_col, jnp.minimum(drawn[..., 1], TILE - W), drawn[..., 1])
    return jnp.stack([row_corner, col_corner], -1).astype(jnp.int32)


def draw_counts(key, part):
    column_keys = jax.random.split(key, COL_TILES)

    def draw_column(column_key):
        order_key, count_key = jax.random.split(column_key)
        ordering = jax.random.permutation(order_key, ROW_TILES)
        first_counts = jax.random.randint(count_key, (ROW_TILES // 2,), 0, SLOTS + 1)
        first_counts = first_counts.at[0].set(SLOTS)
        paired = jnp.stack([first_counts, SLOTS - first_counts], 1).reshape(-1).astype(jnp.int32)
        return jnp.zeros((ROW_TILES,), jnp.int32).at[ordering].set(paired)
    return jax.vmap(draw_column)(column_keys).T


def block_scale(key, shape, cuts, least, high):
    loudness = 1.0
    for dim, shards_of in cuts:
        draws = jax.random.uniform(jax.random.fold_in(jax.random.fold_in(key, 6), dim), (shards_of,), jnp.float32, least / len(cuts), high / len(cuts))
        loudness = loudness * jnp.repeat(jnp.exp(draws), shape[dim] // shards_of).reshape((-1,) + (1,) * (len(shape) - 1 - dim))
    return loudness


def scatter_about(stream_key, shape, width, bound, kind=jnp.bfloat16):
    entries = width * jax.random.normal(stream_key, shape, jnp.float32)
    return jnp.clip(entries, min=-bound, max=bound).astype(kind)


def setup_inputs(seed: int = 0) -> dict:
    splits = jax.random.split(jax.random.key(seed), 7)
    object_field = draw_object_field(jax.random.fold_in(splits[6], 71), 0)
    probe_field = scatter_about(splits[1], (2, W, W), 0.35, 2.1, jnp.float32)
    corners = draw_corners(jax.random.fold_in(splits[6], 71), 0)
    counts = draw_counts(jax.random.fold_in(splits[6], 71), 0)
    intensity = jnp.clip(1.5 * jax.random.uniform(splits[4], (ROW_TILES, COL_TILES, SLOTS, W, W), jnp.float32) ** block_scale(splits[4], (ROW_TILES, COL_TILES, SLOTS, W, W), ((0, 4), (1, 8)), -0.2, 0.2), 0.0, 1.5).astype(jnp.bfloat16)
    damping = jnp.clip(jnp.exp(jax.random.uniform(splits[5], (), jnp.float32, math.log(0.5), math.log(4.0))), 0.5, 4.0)
    return {"object_field": object_field, "probe_field": probe_field, "corners": corners, "counts": counts, "intensity": intensity, "damping": damping}


def make_table(extent, direction_sign):
    indices = jnp.arange(extent, dtype=jnp.int32)
    phases = ((indices[:, None] * indices[None, :]) % extent).astype(jnp.float32)
    angles = phases * (2.0 * jnp.pi / extent)
    norm_scale = 1.0 / float(extent) ** 0.5
    cosine = jnp.cos(angles) * norm_scale
    sines = direction_sign * jnp.sin(angles) * norm_scale
    tables = jnp.stack([jnp.stack([cosine, sines], 1), jnp.stack([-sines, cosine], 1)], 0)
    return tables.astype(jnp.bfloat16)


def transform(field, tables):
    halfway = jnp.einsum("btrc,tcsk->bsrk", field.astype(jnp.float32), tables.astype(jnp.float32))
    halfway = halfway.astype(jnp.bfloat16)
    return jnp.einsum("btrc,trsk->bskc", halfway.astype(jnp.float32), tables.astype(jnp.float32))


def times_probe(probe_field, patches):
    real_part = probe_field[0] * patches[:, 0] - probe_field[1] * patches[:, 1]
    imag_part = probe_field[0] * patches[:, 1] + probe_field[1] * patches[:, 0]
    return jnp.stack([real_part, imag_part], 1)


def times_conj_probe(probe_field, returned):
    real_part = probe_field[0] * returned[:, 0] + probe_field[1] * returned[:, 1]
    imag_part = probe_field[0] * returned[:, 1] - probe_field[1] * returned[:, 0]
    return jnp.stack([real_part, imag_part], 1)


def reference(object_field, probe_field, corners, counts, intensity, damping):
    extent = probe_field.shape[-1]
    forward = make_table(extent, -1.0)
    inverse = make_table(extent, 1.0)
    slot_ids = jnp.arange(SLOTS, dtype=jnp.int32)
    alive_mask = (slot_ids[None, None, :] < counts[:, :, None]).reshape(-1)
    tile_rows = jnp.arange(ROW_TILES, dtype=jnp.int32)[:, None, None] * TILE
    tile_cols = jnp.arange(COL_TILES, dtype=jnp.int32)[None, :, None] * TILE
    corner_rows = (corners[..., 0] + tile_rows).reshape(-1).astype(jnp.int32)
    corner_cols = (corners[..., 1] + tile_cols).reshape(-1).astype(jnp.int32)
    chosen = jnp.nonzero(alive_mask, size=POSITIONS)[0].astype(jnp.int32)
    corner_rows = corner_rows[chosen]
    corner_cols = corner_cols[chosen]
    measured = intensity.reshape(-1, extent, extent)[chosen]
    group_len = 8
    block_count = POSITIONS // group_len
    block_items = (corner_rows.reshape(block_count, group_len), corner_cols.reshape(block_count, group_len), measured.reshape(block_count, group_len, extent, extent))

    def cut_window(field, row_at, col_at):
        anchor = jnp.zeros((), jnp.int32)
        return lax.dynamic_slice(field, (anchor, row_at, col_at), (2, extent, extent))

    def sweep_all(direction):
        def block_step(totals, items):
            block_rows, block_cols, block_data = items
            patches = jax.vmap(lambda r, c: cut_window(object_field, r, c))(block_rows, block_cols)
            exit_wave = times_probe(probe_field, patches.astype(jnp.float32)).astype(jnp.bfloat16)
            far_field = transform(exit_wave, forward)
            if direction is None:
                powers = far_field[:, 0] * far_field[:, 0] + far_field[:, 1] * far_field[:, 1]
                misfit = powers - block_data.astype(jnp.float32)
                mixture = far_field * misfit[:, None]
                weight_factor = 2.0
            else:
                moved = jax.vmap(lambda r, c: cut_window(direction, r, c))(block_rows, block_cols)
                moved_wave = times_probe(probe_field, moved.astype(jnp.float32)).astype(jnp.bfloat16)
                image_field = transform(moved_wave, forward)
                projected = far_field[:, 0] * image_field[:, 0] + far_field[:, 1] * image_field[:, 1]
                mixture = far_field * projected[:, None]
                weight_factor = 4.0
            returned = transform(mixture.astype(jnp.bfloat16), inverse).astype(jnp.bfloat16)
            contribs = weight_factor * times_conj_probe(probe_field, returned.astype(jnp.float32))

            def add_patch(k, running):
                anchor = jnp.zeros((), jnp.int32)
                previous = lax.dynamic_slice(running, (anchor, block_rows[k], block_cols[k]), (2, extent, extent))
                return lax.dynamic_update_slice(running, previous + contribs[k], (anchor, block_rows[k], block_cols[k]))

            return lax.fori_loop(0, group_len, add_patch, totals), None

        initial = jnp.zeros(object_field.shape, jnp.float32)
        totals, _ = lax.scan(block_step, initial, block_items)
        return totals

    gradient = sweep_all(None)
    residual = -gradient
    direction = residual
    solution = jnp.zeros_like(gradient)
    norm_now = jnp.sum(residual * residual)
    for step in range(ITERS):
        image_field = sweep_all(direction.astype(jnp.bfloat16)) + damping * direction
        step_len = norm_now / jnp.sum(direction * image_field)
        solution = solution + step_len * direction
        residual = residual - step_len * image_field
        norm_next = jnp.sum(residual * residual)
        direction = residual + (norm_next / norm_now) * direction
        norm_now = norm_next
    return solution
```

```python
import functools

import jax
import jax.numpy as jnp
import numpy as np
from jax import lax
from jax.experimental import pallas as pl
from jax.experimental.pallas import tpu as pltpu
from jax.sharding import PartitionSpec as P

MESH = pl.DeviceIdType.MESH
LANES = 128
SCALE = 2.0**-24
CHUNKS = 4
F32 = jnp.float32
BF16 = jnp.bfloat16
VMEM_SPEC = pl.BlockSpec(memory_space=pltpu.VMEM)
SMEM_SPEC = pl.BlockSpec(memory_space=pltpu.SMEM)


def make_table(extent, direction_sign):
    indices = np.arange(extent)
    angles = (indices[:, None] * indices[None, :] % extent) * (2.0 * np.pi / extent)
    cosine = np.cos(angles) / extent**0.5
    sines = direction_sign * np.sin(angles) / extent**0.5
    table = np.block([[cosine, sines], [-sines, cosine]])
    return jnp.asarray(table.astype(np.float32)).astype(BF16)


def place():
    ty, tx = lax.axis_index("ty"), lax.axis_index("tx")
    return ty, tx, ty > 0, ty < lax.axis_size("ty") - 1, tx > 0, tx < lax.axis_size("tx") - 1


def greet_neighbours():
    ty, tx, has_up, has_down, has_left, has_right = place()
    barrier = pltpu.get_barrier_semaphore()
    sides = (
        (has_up, {"ty": ty - 1}),
        (has_down, {"ty": ty + 1}),
        (has_left, {"tx": tx - 1}),
        (has_right, {"tx": tx + 1}),
    )
    for present, peer in sides:
        @pl.when(present)
        def _():
            pl.semaphore_signal(barrier, inc=1, device_id=peer, device_id_type=MESH)
    pl.semaphore_wait(barrier, sum(present.astype(jnp.int32) for present, _ in sides))


def remote(src, dst, send_sem, recv_sem, index, peer):
    return pltpu.make_async_remote_copy(
        src_ref=src,
        dst_ref=dst,
        send_sem=send_sem.at[index],
        recv_sem=recv_sem.at[index],
        device_id=peer,
        device_id_type=MESH,
    )


def rows_of(chunk, extent):
    size = extent // CHUNKS
    return pl.ds(chunk * size, size)


def margin_copies(out_left, in_right, own, right, below, corner, send_sem, recv_sem, base):
    ty, tx = place()[:2]
    to_left, to_up, on_up = [], [], []
    for c in range(CHUNKS):
        rows = rows_of(c, own.shape[2])
        part = [ref.at[:, :, rows] for ref in (out_left, in_right, own, right, below, corner)]
        to_left.append(remote(part[0], part[1], send_sem, recv_sem, base + 3 * c, {"tx": tx - 1}))
        to_up.append(remote(part[2], part[4], send_sem, recv_sem, base + 3 * c + 1, {"ty": ty - 1}))
        on_up.append(remote(part[3], part[5], send_sem, recv_sem, base + 3 * c + 2, {"ty": ty - 1}))
    return to_left, to_up, on_up


def start_if(present, copy):
    @pl.when(present)
    def _():
        copy.start()


def take_right(copies, c, on_arrival):
    ty, tx, has_up, has_down, has_left, has_right = place()

    @pl.when(has_right)
    def _():
        copies[0][c].wait_recv()
        on_arrival()

        @pl.when(has_up)
        def _():
            copies[2][c].start()


def settle_margins(copies):
    ty, tx, has_up, has_down, has_left, has_right = place()
    to_left, to_up, on_up = copies

    @pl.when(has_down)
    def _():
        for copy in to_up:
            copy.wait_recv()

        @pl.when(has_right)
        def _():
            for copy in on_up:
                copy.wait_recv()

    @pl.when(has_left)
    def _():
        for copy in to_left:
            copy.wait_send()

    @pl.when(has_up)
    def _():
        for copy in to_up:
            copy.wait_send()

        @pl.when(has_right)
        def _():
            for copy in on_up:
                copy.wait_send()


def lane_sums(values):
    return jnp.sum(values.reshape(-1, LANES), 0, keepdims=True)


def fold_margins(top, bottom, inbox_far, inbox_near, outbox, inbox_side, total, beside, send_sem, recv_sem,
                 before_sum, after_sum):
    ty, tx, has_up, has_down, has_left, has_right = place()
    far, near, side, spans = [], [], [], []
    for c in range(CHUNKS):
        rows = rows_of(c, total.shape[2])
        spans.append(rows)
        far.append(remote(
            bottom.at[pl.ds(2, 2), :, rows], inbox_far.at[:, :, rows], send_sem, recv_sem, 3 * c, {"ty": ty + 1}
        ))
        near.append(remote(
            bottom.at[pl.ds(0, 2), :, rows], inbox_near.at[:, :, rows], send_sem, recv_sem, 3 * c + 1, {"ty": ty + 1}
        ))
        side.append(remote(
            outbox.at[:, :, rows], inbox_side.at[:, :, rows], send_sem, recv_sem, 3 * c + 2, {"tx": tx + 1}
        ))

    @pl.when(has_down)
    def _():
        for c in range(CHUNKS):
            far[c].start()
            near[c].start()

    for c in range(CHUNKS):
        rows = spans[c]

        @pl.when(has_up)
        def _():
            far[c].wait_recv()
            near[c].wait_recv()
            beside[:, :, rows] = top[2:4, :, rows] + inbox_far[:, :, rows].astype(F32)
            total[:, :, rows] = top[0:2, :, rows] + inbox_near[:, :, rows].astype(F32)

        @pl.when(ty == 0)
        def _():
            beside[:, :, rows] = top[2:4, :, rows]
            total[:, :, rows] = top[0:2, :, rows]

        @pl.when(has_right)
        def _():
            outbox[:, :, rows] = beside[:, :, rows].astype(BF16)
            side[c].start()

        before_sum(c, rows)

    for c in range(CHUNKS):
        @pl.when(has_left)
        def _():
            side[c].wait_recv()
            total[:, :, spans[c]] += inbox_side[:, :, spans[c]].astype(F32)

        after_sum(c, spans[c])

    @pl.when(has_down)
    def _():
        for copy in far + near:
            copy.wait_send()

    @pl.when(has_right)
    def _():
        for copy in side:
            copy.wait_send()


def spread_kernel(object_ref, own, right, below, corner, send_sem, recv_sem):
    for h in range(2):
        for t in range(2):
            own[h, t] = object_ref[t, :, h * LANES:(h + 1) * LANES]
    greet_neighbours()
    copies = margin_copies(own, right, own, right, below, corner, send_sem, recv_sem, 0)
    has_up, has_left = place()[2], place()[4]
    for c in range(CHUNKS):
        start_if(has_left, copies[0][c])
        start_if(has_up, copies[1][c])
    for c in range(CHUNKS):
        take_right(copies, c, lambda: None)
    settle_margins(copies)


def exchange_kernel(first, *refs):
    if first:
        top, bottom = refs[:2]
        refs = refs[2:]
    else:
        damping, top, bottom, before, before_right = refs[:5]
        refs = refs[5:]
    q_ref, q_right, own, right, below, corner = refs[:6]
    boxes, (out_left, in_right, send_sem, recv_sem) = refs[6:12], refs[12:]
    total, beside = boxes[-2:]
    has_up, has_left = place()[2], place()[4]
    greet_neighbours()
    copies = margin_copies(out_left, in_right, own, right, below, corner, send_sem, recv_sem, 3 * CHUNKS)

    def scaled(sums, old, rows):
        if first:
            return -2.0 * sums
        return (4.0 * SCALE) * sums + (damping[0] * SCALE) * old[:, :, rows]

    def send_part(c, rows):
        @pl.when(has_left)
        def _():
            out_left[:, :, rows] = total[:, :, rows].astype(BF16)
            copies[0][c].start()

    def use(c, rows):
        q = scaled(total[:, :, rows], None if first else before, rows)
        q_ref[:, :, rows] = q
        own[:, :, rows] = q.astype(BF16)
        start_if(has_up, copies[1][c])

        def on_arrival():
            sums = beside[:, :, rows] + in_right[:, :, rows].astype(F32)
            q = scaled(sums, None if first else before_right, rows)
            q_right[:, :, rows] = q
            right[:, :, rows] = q.astype(BF16)

        take_right(copies, c, on_arrival)

    fold_margins(top, bottom, *boxes, send_sem, recv_sem, send_part, use)
    settle_margins(copies)


def finish_kernel(damping, energy0, energy1, q0_ref, q1_ref, out_ref, sums_y, sums_x, send_y, recv_y, send_x, recv_x):
    ty, tx = place()[:2]
    n_y, n_x = lax.axis_size("ty"), lax.axis_size("tx")
    barrier = pltpu.get_barrier_semaphore()
    for axis, me, n in (("ty", ty, n_y), ("tx", tx, n_x)):
        for step in range(1, n):
            pl.semaphore_signal(
                barrier, inc=1, device_id={axis: lax.rem(me + step, n)}, device_id_type=MESH
            )
    q0, q1 = q0_ref[...], q1_ref[...]
    rows = [lane_sums(q0 * q0), lane_sums(q1 * q1), lane_sums(energy0[...]), lane_sums(energy1[...])]
    partial = jnp.concatenate(rows + [jnp.zeros((4, LANES), F32)], 0)
    pl.semaphore_wait(barrier, n_y + n_x - 2)

    def reduce_over(partial, sums, send, recv, axis, me, n):
        sums[me] = partial
        copies = []
        for step in range(1, n):
            copies.append(pltpu.make_async_remote_copy(
                src_ref=sums.at[me], dst_ref=sums.at[me],
                send_sem=send.at[step], recv_sem=recv.at[step],
                device_id={axis: lax.rem(me + step, n)}, device_id_type=MESH,
            ))
        for copy in copies:
            copy.start()
        for copy in copies:
            copy.wait()
        return jnp.sum(sums[...], 0)

    partial = reduce_over(partial, sums_y, send_y, recv_y, "ty", ty, n_y)
    partial = reduce_over(partial, sums_x, send_x, recv_x, "tx", tx, n_x)
    dots = jnp.sum(partial, 1, keepdims=True)
    rr, s11, w00, w11 = (dots[k:k + 1] for k in range(4))
    c01 = SCALE * (4.0 * w00 + damping[0] * rr)
    s12 = SCALE * (4.0 * w11 + damping[0] * s11)
    alpha = rr / c01
    rr_next = rr - 2.0 * alpha * c01 + alpha * alpha * s11
    gain = 1.0 + rr_next / rr
    curvature = gain * gain * c01 - 2.0 * gain * alpha * s11 + alpha * alpha * s12
    step_len = rr_next / curvature
    first = (alpha + step_len * gain) * SCALE
    second = step_len * alpha * SCALE
    for h in range(2):
        for t in range(2):
            out_ref[t, :, h * LANES:(h + 1) * LANES] = first * q0_ref[h, t] - second * q1_ref[h, t]


def sweep_kernel(kind, group, corners, count, own, right, below, corner, probe, table_f, table_g, extra, *rest):
    first, last = kind == "first", kind == "last"
    if first:
        top, bottom, psi_ref, turned, field, total = rest
    elif last:
        energy, field = rest
    else:
        top, bottom, energy, field, total = rest
    if not first:
        psi_ref, turned = extra, probe
        energy[...] = jnp.zeros_like(energy)
    extent = probe.shape[-2]
    tile = own.shape[2]
    field[0:2, :, 0:tile] = own[...].astype(F32)
    field[2:4, :, 0:tile] = right[...].astype(F32)
    field[0:2, :, tile:] = below[...].astype(F32)
    field[2:4, :, tile:] = corner[...].astype(F32)
    if not last:
        total[...] = jnp.zeros_like(total)
    lane = lax.broadcasted_iota(jnp.int32, (extent, LANES), 1)
    live = count[0]

    def turn_probe(s):
        shift = lax.rem(corners[1, s], LANES)
        keep = lane >= shift
        for t in range(2):
            near = pltpu.roll(probe[t, :, 0:LANES], shift, 1)
            far = pltpu.roll(probe[t, :, LANES:], shift, 1)
            turned[s, t, :, 0:LANES] = jnp.where(keep, near, far)
            turned[s, t, :, LANES:] = jnp.where(keep, far, near)

    def cut(s):
        row, col = corners[0, s], corners[1, s]
        block, shift = col // LANES, lax.rem(col, LANES)
        keep = lane >= shift
        rows = pl.ds(row, extent)
        waves = [[], []]
        for k in range(2):
            halves = []
            for t in range(2):
                if k == 0:
                    halves.append(jnp.where(keep, field[block, t, rows, :], field[block + 2, t, rows, :]))
                else:
                    halves.append(field[block + 1, t, rows, :])
            lanes = slice(k * LANES, (k + 1) * LANES)
            probe_re, probe_im = turned[s, 0, :, lanes], turned[s, 1, :, lanes]
            waves[0].append((probe_re * halves[0] - probe_im * halves[1]).astype(BF16))
            waves[1].append((probe_re * halves[1] + probe_im * halves[0]).astype(BF16))
        return jnp.concatenate(waves[0] + waves[1], 1)

    def add(s, back):
        row, col = corners[0, s], corners[1, s]
        block, shift = col // LANES, lax.rem(col, LANES)
        keep = lane >= shift
        rows = pl.ds(row, extent)
        for k in range(2):
            lanes = slice(k * LANES, (k + 1) * LANES)
            probe_re, probe_im = turned[s, 0, :, lanes], turned[s, 1, :, lanes]
            re, im = back[:extent, lanes], back[extent:, lanes]
            for t in range(2):
                if t == 0:
                    term = probe_re * re + probe_im * im
                else:
                    term = probe_re * im - probe_im * re
                if k == 0:
                    zero = jnp.zeros_like(term)
                    total[block, t, rows, :] += jnp.where(keep, term, zero)
                    total[block + 2, t, rows, :] += jnp.where(keep, zero, term)
                else:
                    total[block + 1, t, rows, :] += term

    def transform(waves, rhs, lhs):
        half = jnp.dot(waves, rhs[...], preferred_element_type=F32).astype(BF16)
        columns = []
        for g in range(group):
            part = half[g * extent:(g + 1) * extent]
            columns.append(jnp.concatenate([part[:, :extent], part[:, extent:]], 0))
        return jnp.dot(lhs[...], jnp.concatenate(columns, 1), preferred_element_type=F32)

    def step(index, carry):
        base = index * group
        if first:
            for g in range(group):
                turn_probe(base + g)
        waves = jnp.concatenate([cut(base + g) for g in range(group)], 0)
        image = transform(waves, table_f, table_g)
        mixed = []
        for g in range(group):
            re = image[:extent, g * extent:(g + 1) * extent]
            im = image[extent:, g * extent:(g + 1) * extent]
            if first:
                psi_ref[base + g, 0] = re
                psi_ref[base + g, 1] = im
                weight = re * re + im * im - extra[base + g].astype(F32)
                psi_re, psi_im = re, im
            else:
                psi_re, psi_im = psi_ref[base + g, 0], psi_ref[base + g, 1]
                weight = psi_re * re + psi_im * im
                squares = jnp.sum((weight * weight).reshape(-1, 8, LANES), 0)
                energy[...] += jnp.where(base + g < live, squares, jnp.zeros_like(squares))
            if last:
                continue
            mixed.append(jnp.concatenate([(psi_re * weight).astype(BF16), (psi_im * weight).astype(BF16)], 1))
        if last:
            return carry
        back = transform(jnp.concatenate(mixed, 0), table_g, table_f)
        for g in range(group):
            @pl.when(base + g < live)
            def _():
                add(base + g, back[:, g * extent:(g + 1) * extent])
        return carry

    lax.fori_loop(0, (live + group - 1) // group, step, 0)
    if not last:
        top[...] = total[:, :, 0:tile]
        bottom[...] = total[:, :, tile:].astype(BF16)


def per_device(object_field, probe_field, corners, counts, intensity, damping):
    extent = probe_field.shape[-1]
    tile = object_field.shape[1]
    slots = corners.shape[2]
    group = min(4, slots)
    n_y, n_x = lax.axis_size("ty"), lax.axis_size("tx")
    places = corners.reshape(slots, 2).T
    count = counts.reshape(1)
    measured = intensity.reshape(slots, extent, extent)
    damping = damping.reshape(1)
    table_f, table_g = make_table(extent, -1.0), make_table(extent, 1.0)

    def shaped(shape, dtype):
        return jax.ShapeDtypeStruct(shape, dtype)

    quarter = (2, 2, tile, LANES)
    quarters = [shaped(quarter, BF16)] * 4
    boxes = [pltpu.VMEM(quarter, BF16)] * 4 + [pltpu.VMEM(quarter, F32)] * 2

    def sems(n):
        return [pltpu.SemaphoreType.DMA((n,)), pltpu.SemaphoreType.DMA((n,))]

    def params(collective_id):
        return pltpu.CompilerParams(
            collective_id=collective_id, has_side_effects=True, vmem_limit_bytes=16 << 20
        )

    margins = pl.pallas_call(
        spread_kernel,
        out_shape=quarters,
        in_specs=[VMEM_SPEC],
        out_specs=[VMEM_SPEC] * 4,
        scratch_shapes=sems(3 * CHUNKS),
        compiler_params=params(0),
        cost_estimate=pl.CostEstimate(flops=10**10, bytes_accessed=30 << 20, transcendentals=0),
        name="spread",
    )(object_field)

    def sweep(margins, probe, extra, kind):
        outs = []
        if kind != "last":
            outs += [shaped((4, 2, tile, LANES), F32), shaped((4, 2, tile, LANES), BF16)]
        if kind == "first":
            outs += [shaped((slots, 2, extent, extent), F32)] * 2
        else:
            outs += [shaped((8, LANES), F32)]
        return pl.pallas_call(
            functools.partial(sweep_kernel, kind, group),
            out_shape=outs,
            in_specs=[SMEM_SPEC] * 2 + [VMEM_SPEC] * 8,
            out_specs=[VMEM_SPEC] * len(outs),
            scratch_shapes=[pltpu.VMEM((4, 2, 2 * tile, LANES), F32)] * (1 if kind == "last" else 2),
            compiler_params=pltpu.CompilerParams(vmem_limit_bytes=36 << 20),
            name="sweep_" + kind,
        )(places, count, *margins, probe, table_f, table_g, extra)

    top, bottom, psi, turned = sweep(margins, probe_field, measured, "first")
    q0, q0_right, *margins = pl.pallas_call(
        functools.partial(exchange_kernel, True),
        out_shape=[shaped(quarter, F32)] * 2 + quarters,
        in_specs=[VMEM_SPEC] * 2,
        out_specs=[VMEM_SPEC] * 6,
        scratch_shapes=boxes + [pltpu.VMEM(quarter, BF16)] * 2 + sems(6 * CHUNKS),
        compiler_params=params(1),
        name="exchange_first",
    )(top, bottom)
    top, bottom, energy0 = sweep(margins, turned, psi, "middle")
    q1, _, *margins = pl.pallas_call(
        functools.partial(exchange_kernel, False),
        out_shape=[shaped(quarter, F32)] * 2 + quarters,
        in_specs=[SMEM_SPEC] + [VMEM_SPEC] * 4,
        out_specs=[VMEM_SPEC] * 6,
        scratch_shapes=boxes + [pltpu.VMEM(quarter, BF16)] * 2 + sems(6 * CHUNKS),
        compiler_params=params(2),
        name="exchange",
    )(damping, top, bottom, q0, q0_right)
    energy1, = sweep(margins, turned, psi, "last")
    return pl.pallas_call(
        finish_kernel,
        out_shape=shaped((2, tile, tile), F32),
        in_specs=[SMEM_SPEC] + [VMEM_SPEC] * 4,
        out_specs=VMEM_SPEC,
        scratch_shapes=[pltpu.VMEM((n_y, 8, LANES), F32), pltpu.VMEM((n_x, 8, LANES), F32)] + sems(n_y) + sems(n_x),
        compiler_params=params(3),
        name="finish",
    )(damping, energy0, energy1, q0, q1)


def solution(mesh):
    in_specs = (
        P(None, "ty", "tx"),
        P(),
        P("ty", "tx", None, None),
        P("ty", "tx"),
        P("ty", "tx", None, None, None),
        P(),
    )
    out_specs = P(None, "ty", "tx")
    return jax.shard_map(
        per_device, mesh=mesh, in_specs=in_specs, out_specs=out_specs, check_vma=False
    )
```

```python
import functools

import jax
import jax.numpy as jnp
import numpy as np
from jax import lax
from jax.experimental import pallas as pl
from jax.experimental.pallas import tpu as pltpu
from jax.sharding import PartitionSpec as P

MESH = pl.DeviceIdType.MESH
LANES = 128
SCALE = 2.0**-24
CHUNKS = 4
F32 = jnp.float32
BF16 = jnp.bfloat16
VMEM_SPEC = pl.BlockSpec(memory_space=pltpu.VMEM)
SMEM_SPEC = pl.BlockSpec(memory_space=pltpu.SMEM)


def make_table(extent, direction_sign):
    indices = np.arange(extent)
    angles = (indices[:, None] * indices[None, :] % extent) * (2.0 * np.pi / extent)
    cosine = np.cos(angles) / extent**0.5
    sines = direction_sign * np.sin(angles) / extent**0.5
    table = np.block([[cosine, sines], [-sines, cosine]])
    return jnp.asarray(table.astype(np.float32)).astype(BF16)


def place():
    ty, tx = lax.axis_index("ty"), lax.axis_index("tx")
    return ty, tx, ty > 0, ty < lax.axis_size("ty") - 1, tx > 0, tx < lax.axis_size("tx") - 1


def greet_neighbours():
    ty, tx, has_up, has_down, has_left, has_right = place()
    barrier = pltpu.get_barrier_semaphore()
    sides = (
        (has_up, {"ty": ty - 1}),
        (has_down, {"ty": ty + 1}),
        (has_left, {"tx": tx - 1}),
        (has_right, {"tx": tx + 1}),
    )
    for present, peer in sides:
        @pl.when(present)
        def _():
            pl.semaphore_signal(barrier, inc=1, device_id=peer, device_id_type=MESH)
    pl.semaphore_wait(barrier, sum(present.astype(jnp.int32) for present, _ in sides))


def remote(src, dst, send_sem, recv_sem, index, peer):
    return pltpu.make_async_remote_copy(
        src_ref=src,
        dst_ref=dst,
        send_sem=send_sem.at[index],
        recv_sem=recv_sem.at[index],
        device_id=peer,
        device_id_type=MESH,
    )


def rows_of(chunk, extent):
    size = extent // CHUNKS
    return pl.ds(chunk * size, size)


def margin_copies(out_left, in_right, own, right, below, corner, send_sem, recv_sem, base):
    ty, tx = place()[:2]
    to_left, to_up, on_up = [], [], []
    for c in range(CHUNKS):
        rows = rows_of(c, own.shape[2])
        part = [ref.at[:, :, rows] for ref in (out_left, in_right, own, right, below, corner)]
        to_left.append(remote(part[0], part[1], send_sem, recv_sem, base + 3 * c, {"tx": tx - 1}))
        to_up.append(remote(part[2], part[4], send_sem, recv_sem, base + 3 * c + 1, {"ty": ty - 1}))
        on_up.append(remote(part[3], part[5], send_sem, recv_sem, base + 3 * c + 2, {"ty": ty - 1}))
    return to_left, to_up, on_up


def start_if(present, copy):
    @pl.when(present)
    def _():
        copy.start()


def take_right(copies, c, on_arrival):
    ty, tx, has_up, has_down, has_left, has_right = place()

    @pl.when(has_right)
    def _():
        copies[0][c].wait_recv()
        on_arrival()

        @pl.when(has_up)
        def _():
            copies[2][c].start()


def settle_margins(copies):
    ty, tx, has_up, has_down, has_left, has_right = place()
    to_left, to_up, on_up = copies

    @pl.when(has_down)
    def _():
        for copy in to_up:
            copy.wait_recv()

        @pl.when(has_right)
        def _():
            for copy in on_up:
                copy.wait_recv()

    @pl.when(has_left)
    def _():
        for copy in to_left:
            copy.wait_send()

    @pl.when(has_up)
    def _():
        for copy in to_up:
            copy.wait_send()

        @pl.when(has_right)
        def _():
            for copy in on_up:
                copy.wait_send()


def lane_sums(values):
    return jnp.sum(values.reshape(-1, LANES), 0, keepdims=True)


def fold_margins(top, bottom, inbox_far, inbox_near, outbox, inbox_side, total, beside, send_sem, recv_sem,
                 before_sum, after_sum):
    ty, tx, has_up, has_down, has_left, has_right = place()
    far, near, side, spans = [], [], [], []
    for c in range(CHUNKS):
        rows = rows_of(c, total.shape[2])
        spans.append(rows)
        far.append(remote(
            bottom.at[pl.ds(2, 2), :, rows], inbox_far.at[:, :, rows], send_sem, recv_sem, 3 * c, {"ty": ty + 1}
        ))
        near.append(remote(
            bottom.at[pl.ds(0, 2), :, rows], inbox_near.at[:, :, rows], send_sem, recv_sem, 3 * c + 1, {"ty": ty + 1}
        ))
        side.append(remote(
            outbox.at[:, :, rows], inbox_side.at[:, :, rows], send_sem, recv_sem, 3 * c + 2, {"tx": tx + 1}
        ))

    @pl.when(has_down)
    def _():
        for c in range(CHUNKS):
            far[c].start()
            near[c].start()

    for c in range(CHUNKS):
        rows = spans[c]

        @pl.when(has_up)
        def _():
            far[c].wait_recv()
            near[c].wait_recv()
            beside[:, :, rows] = top[2:4, :, rows] + inbox_far[:, :, rows].astype(F32)
            total[:, :, rows] = top[0:2, :, rows] + inbox_near[:, :, rows].astype(F32)

        @pl.when(ty == 0)
        def _():
            beside[:, :, rows] = top[2:4, :, rows]
            total[:, :, rows] = top[0:2, :, rows]

        @pl.when(has_right)
        def _():
            outbox[:, :, rows] = beside[:, :, rows].astype(BF16)
            side[c].start()

        before_sum(c, rows)

    for c in range(CHUNKS):
        @pl.when(has_left)
        def _():
            side[c].wait_recv()
            total[:, :, spans[c]] += inbox_side[:, :, spans[c]].astype(F32)

        after_sum(c, spans[c])

    @pl.when(has_down)
    def _():
        for copy in far + near:
            copy.wait_send()

    @pl.when(has_right)
    def _():
        for copy in side:
            copy.wait_send()


def spread_kernel(object_ref, own, right, below, corner, send_sem, recv_sem):
    for h in range(2):
        for t in range(2):
            own[h, t] = object_ref[t, :, h * LANES:(h + 1) * LANES]
    greet_neighbours()
    copies = margin_copies(own, right, own, right, below, corner, send_sem, recv_sem, 0)
    has_up, has_left = place()[2], place()[4]
    for c in range(CHUNKS):
        start_if(has_left, copies[0][c])
        start_if(has_up, copies[1][c])
    for c in range(CHUNKS):
        take_right(copies, c, lambda: None)
    settle_margins(copies)


def exchange_kernel(first, *refs):
    if first:
        top, bottom = refs[:2]
        refs = refs[2:]
    else:
        damping, top, bottom, before, before_right = refs[:5]
        refs = refs[5:]
    q_ref, q_right, own, right, below, corner = refs[:6]
    boxes, (out_left, in_right, send_sem, recv_sem) = refs[6:12], refs[12:]
    total, beside = boxes[-2:]
    has_up, has_left = place()[2], place()[4]
    greet_neighbours()
    copies = margin_copies(out_left, in_right, own, right, below, corner, send_sem, recv_sem, 3 * CHUNKS)

    def scaled(sums, old, rows):
        if first:
            return -2.0 * sums
        return (4.0 * SCALE) * sums + (damping[0] * SCALE) * old[:, :, rows]

    def send_part(c, rows):
        @pl.when(has_left)
        def _():
            out_left[:, :, rows] = total[:, :, rows].astype(BF16)
            copies[0][c].start()

    def use(c, rows):
        q = scaled(total[:, :, rows], None if first else before, rows)
        q_ref[:, :, rows] = q
        own[:, :, rows] = q.astype(BF16)
        start_if(has_up, copies[1][c])

        def on_arrival():
            sums = beside[:, :, rows] + in_right[:, :, rows].astype(F32)
            q = scaled(sums, None if first else before_right, rows)
            q_right[:, :, rows] = q
            right[:, :, rows] = q.astype(BF16)

        take_right(copies, c, on_arrival)

    fold_margins(top, bottom, *boxes, send_sem, recv_sem, send_part, use)
    settle_margins(copies)


def finish_kernel(group, corners, count, damping, own, right, below, corner, turned, table_f, table_g, psi_ref, energy0, q0_ref, q1_ref,
                  out_ref, field, energy1, sums_y, sums_x, send_y, recv_y, send_x, recv_x):
    ty, tx = place()[:2]
    n_y, n_x = lax.axis_size("ty"), lax.axis_size("tx")
    barrier = pltpu.get_barrier_semaphore()
    for axis, me, n in (("ty", ty, n_y), ("tx", tx, n_x)):
        for step in range(1, n):
            pl.semaphore_signal(
                barrier, inc=1, device_id={axis: lax.rem(me + step, n)}, device_id_type=MESH
            )
    sweep_kernel("last", group, corners, count, own, right, below, corner, turned, table_f, table_g, psi_ref, energy1, field)
    q0, q1 = q0_ref[...], q1_ref[...]
    rows = [lane_sums(q0 * q0), lane_sums(q1 * q1), lane_sums(energy0[...]), lane_sums(energy1[...])]
    partial = jnp.concatenate(rows + [jnp.zeros((4, LANES), F32)], 0)
    pl.semaphore_wait(barrier, n_y + n_x - 2)

    def reduce_over(partial, sums, send, recv, axis, me, n):
        sums[me] = partial
        copies = []
        for step in range(1, n):
            copies.append(pltpu.make_async_remote_copy(
                src_ref=sums.at[me], dst_ref=sums.at[me],
                send_sem=send.at[step], recv_sem=recv.at[step],
                device_id={axis: lax.rem(me + step, n)}, device_id_type=MESH,
            ))
        for copy in copies:
            copy.start()
        for copy in copies:
            copy.wait()
        return jnp.sum(sums[...], 0)

    partial = reduce_over(partial, sums_y, send_y, recv_y, "ty", ty, n_y)
    partial = reduce_over(partial, sums_x, send_x, recv_x, "tx", tx, n_x)
    dots = jnp.sum(partial, 1, keepdims=True)
    rr, s11, w00, w11 = (dots[k:k + 1] for k in range(4))
    c01 = SCALE * (4.0 * w00 + damping[0] * rr)
    s12 = SCALE * (4.0 * w11 + damping[0] * s11)
    alpha = rr / c01
    rr_next = rr - 2.0 * alpha * c01 + alpha * alpha * s11
    gain = 1.0 + rr_next / rr
    curvature = gain * gain * c01 - 2.0 * gain * alpha * s11 + alpha * alpha * s12
    step_len = rr_next / curvature
    first = (alpha + step_len * gain) * SCALE
    second = step_len * alpha * SCALE
    for h in range(2):
        for t in range(2):
            out_ref[t, :, h * LANES:(h + 1) * LANES] = first * q0_ref[h, t] - second * q1_ref[h, t]


def sweep_kernel(kind, group, corners, count, own, right, below, corner, probe, table_f, table_g, extra, *rest):
    first, last = kind == "first", kind == "last"
    if first:
        top, bottom, psi_ref, turned, field, total = rest
    elif last:
        energy, field = rest
    else:
        top, bottom, energy, field, total = rest
    if not first:
        psi_ref, turned = extra, probe
        energy[...] = jnp.zeros_like(energy)
    extent = probe.shape[-2]
    tile = own.shape[2]
    field[0:2, :, 0:tile] = own[...].astype(F32)
    field[2:4, :, 0:tile] = right[...].astype(F32)
    field[0:2, :, tile:] = below[...].astype(F32)
    field[2:4, :, tile:] = corner[...].astype(F32)
    if not last:
        total[...] = jnp.zeros_like(total)
    lane = lax.broadcasted_iota(jnp.int32, (extent, LANES), 1)
    live = count[0]

    def turn_probe(s):
        shift = lax.rem(corners[1, s], LANES)
        keep = lane >= shift
        for t in range(2):
            near = pltpu.roll(probe[t, :, 0:LANES], shift, 1)
            far = pltpu.roll(probe[t, :, LANES:], shift, 1)
            turned[s, t, :, 0:LANES] = jnp.where(keep, near, far)
            turned[s, t, :, LANES:] = jnp.where(keep, far, near)

    def cut(s):
        row, col = corners[0, s], corners[1, s]
        block, shift = col // LANES, lax.rem(col, LANES)
        keep = lane >= shift
        rows = pl.ds(row, extent)
        waves = [[], []]
        for k in range(2):
            halves = []
            for t in range(2):
                if k == 0:
                    halves.append(jnp.where(keep, field[block, t, rows, :], field[block + 2, t, rows, :]))
                else:
                    halves.append(field[block + 1, t, rows, :])
            lanes = slice(k * LANES, (k + 1) * LANES)
            probe_re, probe_im = turned[s, 0, :, lanes], turned[s, 1, :, lanes]
            waves[0].append((probe_re * halves[0] - probe_im * halves[1]).astype(BF16))
            waves[1].append((probe_re * halves[1] + probe_im * halves[0]).astype(BF16))
        return jnp.concatenate(waves[0] + waves[1], 1)

    def add(s, back):
        row, col = corners[0, s], corners[1, s]
        block, shift = col // LANES, lax.rem(col, LANES)
        keep = lane >= shift
        rows = pl.ds(row, extent)
        for k in range(2):
            lanes = slice(k * LANES, (k + 1) * LANES)
            probe_re, probe_im = turned[s, 0, :, lanes], turned[s, 1, :, lanes]
            re, im = back[:extent, lanes], back[extent:, lanes]
            for t in range(2):
                if t == 0:
                    term = probe_re * re + probe_im * im
                else:
                    term = probe_re * im - probe_im * re
                if k == 0:
                    zero = jnp.zeros_like(term)
                    total[block, t, rows, :] += jnp.where(keep, term, zero)
                    total[block + 2, t, rows, :] += jnp.where(keep, zero, term)
                else:
                    total[block + 1, t, rows, :] += term

    def transform(waves, rhs, lhs):
        half = jnp.dot(waves, rhs[...], preferred_element_type=F32).astype(BF16)
        columns = []
        for g in range(group):
            part = half[g * extent:(g + 1) * extent]
            columns.append(jnp.concatenate([part[:, :extent], part[:, extent:]], 0))
        return jnp.dot(lhs[...], jnp.concatenate(columns, 1), preferred_element_type=F32)

    def step(index, carry):
        base = index * group
        if first:
            for g in range(group):
                turn_probe(base + g)
        waves = jnp.concatenate([cut(base + g) for g in range(group)], 0)
        image = transform(waves, table_f, table_g)
        mixed = []
        for g in range(group):
            re = image[:extent, g * extent:(g + 1) * extent]
            im = image[extent:, g * extent:(g + 1) * extent]
            if first:
                psi_ref[base + g, 0] = re
                psi_ref[base + g, 1] = im
                weight = re * re + im * im - extra[base + g].astype(F32)
                psi_re, psi_im = re, im
            else:
                psi_re, psi_im = psi_ref[base + g, 0], psi_ref[base + g, 1]
                weight = psi_re * re + psi_im * im
                squares = jnp.sum((weight * weight).reshape(-1, 8, LANES), 0)
                energy[...] += jnp.where(base + g < live, squares, jnp.zeros_like(squares))
            if last:
                continue
            mixed.append(jnp.concatenate([(psi_re * weight).astype(BF16), (psi_im * weight).astype(BF16)], 1))
        if last:
            return carry
        back = transform(jnp.concatenate(mixed, 0), table_g, table_f)
        for g in range(group):
            @pl.when(base + g < live)
            def _():
                add(base + g, back[:, g * extent:(g + 1) * extent])
        return carry

    lax.fori_loop(0, corners.shape[1] // group if last else (live + group - 1) // group, step, 0)
    if not last:
        top[...] = total[:, :, 0:tile]
        bottom[...] = total[:, :, tile:].astype(BF16)


def per_device(object_field, probe_field, corners, counts, intensity, damping):
    extent = probe_field.shape[-1]
    tile = object_field.shape[1]
    slots = corners.shape[2]
    group = 4 if slots % 4 == 0 else 1
    n_y, n_x = lax.axis_size("ty"), lax.axis_size("tx")
    places = corners.reshape(slots, 2).T
    count = counts.reshape(1)
    measured = intensity.reshape(slots, extent, extent)
    damping = damping.reshape(1)
    table_f, table_g = make_table(extent, -1.0), make_table(extent, 1.0)

    def shaped(shape, dtype):
        return jax.ShapeDtypeStruct(shape, dtype)

    quarter = (2, 2, tile, LANES)
    quarters = [shaped(quarter, BF16)] * 4
    boxes = [pltpu.VMEM(quarter, BF16)] * 4 + [pltpu.VMEM(quarter, F32)] * 2

    def sems(n):
        return [pltpu.SemaphoreType.DMA((n,)), pltpu.SemaphoreType.DMA((n,))]

    def params(collective_id):
        return pltpu.CompilerParams(
            collective_id=collective_id, has_side_effects=True, vmem_limit_bytes=16 << 20
        )

    margins = pl.pallas_call(
        spread_kernel,
        out_shape=quarters,
        in_specs=[VMEM_SPEC],
        out_specs=[VMEM_SPEC] * 4,
        scratch_shapes=sems(3 * CHUNKS),
        compiler_params=params(0),
        cost_estimate=pl.CostEstimate(flops=10**10, bytes_accessed=30 << 20, transcendentals=0),
        name="spread",
    )(object_field)

    def sweep(margins, probe, extra, kind):
        outs = []
        if kind != "last":
            outs += [shaped((4, 2, tile, LANES), F32), shaped((4, 2, tile, LANES), BF16)]
        if kind == "first":
            outs += [shaped((slots, 2, extent, extent), F32)] * 2
        else:
            outs += [shaped((8, LANES), F32)]
        return pl.pallas_call(
            functools.partial(sweep_kernel, kind, group),
            out_shape=outs,
            in_specs=[SMEM_SPEC] * 2 + [VMEM_SPEC] * 8,
            out_specs=[VMEM_SPEC] * len(outs),
            scratch_shapes=[pltpu.VMEM((4, 2, 2 * tile, LANES), F32)] * (1 if kind == "last" else 2),
            compiler_params=pltpu.CompilerParams(vmem_limit_bytes=36 << 20),
            name="sweep_" + kind,
        )(places, count, *margins, probe, table_f, table_g, extra)

    top, bottom, psi, turned = sweep(margins, probe_field, measured, "first")
    q0, q0_right, *margins = pl.pallas_call(
        functools.partial(exchange_kernel, True),
        out_shape=[shaped(quarter, F32)] * 2 + quarters,
        in_specs=[VMEM_SPEC] * 2,
        out_specs=[VMEM_SPEC] * 6,
        scratch_shapes=boxes + [pltpu.VMEM(quarter, BF16)] * 2 + sems(6 * CHUNKS),
        compiler_params=params(1),
        name="exchange_first",
    )(top, bottom)
    top, bottom, energy0 = sweep(margins, turned, psi, "middle")
    q1, _, *margins = pl.pallas_call(
        functools.partial(exchange_kernel, False),
        out_shape=[shaped(quarter, F32)] * 2 + quarters,
        in_specs=[SMEM_SPEC] + [VMEM_SPEC] * 4,
        out_specs=[VMEM_SPEC] * 6,
        scratch_shapes=boxes + [pltpu.VMEM(quarter, BF16)] * 2 + sems(6 * CHUNKS),
        compiler_params=params(2),
        name="exchange",
    )(damping, top, bottom, q0, q0_right)
    return pl.pallas_call(
        functools.partial(finish_kernel, group),
        out_shape=shaped((2, tile, tile), F32),
        in_specs=[SMEM_SPEC] * 3 + [VMEM_SPEC] * 11,
        out_specs=VMEM_SPEC,
        scratch_shapes=[pltpu.VMEM((4, 2, 2 * tile, LANES), F32), pltpu.VMEM((8, LANES), F32)]
        + [pltpu.VMEM((n_y, 8, LANES), F32), pltpu.VMEM((n_x, 8, LANES), F32)] + sems(n_y) + sems(n_x),
        compiler_params=pltpu.CompilerParams(collective_id=3, has_side_effects=True, vmem_limit_bytes=36 << 20),
        name="finish",
    )(places, count, damping, *margins, turned, table_f, table_g, psi, energy0, q0, q1)


def solution(mesh):
    in_specs = (
        P(None, "ty", "tx"),
        P(),
        P("ty", "tx", None, None),
        P("ty", "tx"),
        P("ty", "tx", None, None, None),
        P(),
    )
    out_specs = P(None, "ty", "tx")
    return jax.shard_map(
        per_device, mesh=mesh, in_specs=in_specs, out_specs=out_specs, check_vma=False
    )
```

```python
import functools

import jax
import jax.numpy as jnp
import numpy as np
from jax import lax
from jax.experimental import pallas as pl
from jax.experimental.pallas import tpu as pltpu
from jax.sharding import PartitionSpec as P

MESH = pl.DeviceIdType.MESH
LANES = 128
SCALE = 2.0**-24
CHUNKS = 4
F32 = jnp.float32
BF16 = jnp.bfloat16
SMEM_SPEC = pl.BlockSpec(memory_space=pltpu.SMEM)
ANY_SPEC = pl.BlockSpec(memory_space=pl.ANY)


def make_table(extent, direction_sign):
    indices = np.arange(extent)
    angles = (indices[:, None] * indices[None, :] % extent) * (2.0 * np.pi / extent)
    cosine = np.cos(angles) / extent**0.5
    sines = direction_sign * np.sin(angles) / extent**0.5
    table = np.block([[cosine, sines], [-sines, cosine]])
    return jnp.asarray(table.astype(np.float32)).astype(BF16)


def lane_sums(values):
    return jnp.sum(values.reshape(-1, LANES), 0, keepdims=True)


def step_kernel(group, n_y, n_x, corners, count, damping, object_hbm, probe_hbm, measured_hbm, f_hbm, g_hbm, out_ref,
                probe, measured, table_f, table_g, turned, psi_ref, field, patches, total, energy, q, q_right,
                tiles0, tiles1, tiles2, boxes0, boxes1, sums_y, sums_x,
                local_sem, send0, recv0, send1, recv1, send2, recv2, send_y, recv_y, send_x, recv_x):
    slots, extent, tile = turned.shape[0], probe.shape[-1], total.shape[2]
    ty, tx = lax.axis_index("ty"), lax.axis_index("tx")
    has_up, has_down, has_left, has_right = ty > 0, ty < n_y - 1, tx > 0, tx < n_x - 1
    up, down, left, right_peer = {"ty": ty - 1}, {"ty": ty + 1}, {"tx": tx - 1}, {"tx": tx + 1}
    size = tile // CHUNKS
    spans = [pl.ds(c * size, size) for c in range(CHUNKS)]
    lower = [pl.ds(tile + c * size, size) for c in range(CHUNKS)]

    def remote(src, dst, sems, index, peer):
        return pltpu.make_async_remote_copy(
            src_ref=src, dst_ref=dst, send_sem=sems[0].at[index], recv_sem=sems[1].at[index],
            device_id=peer, device_id_type=MESH,
        )

    own0 = tiles0[0]
    fetch = [
        pltpu.make_async_copy(object_hbm.at[t, :, pl.ds(h * LANES, LANES)], own0.at[h, t], local_sem.at[2 * h + t])
        for h in range(2) for t in range(2)
    ]
    later = [
        pltpu.make_async_copy(src, dst, local_sem.at[4 + k])
        for k, (src, dst) in enumerate(
            ((probe_hbm, probe), (f_hbm, table_f), (g_hbm, table_g), (measured_hbm, measured))
        )
    ]
    for copy in fetch + later:
        copy.start()
    barrier = pltpu.get_barrier_semaphore()
    for axis, me, n in (("ty", ty, n_y), ("tx", tx, n_x)):
        for step in range(1, n):
            pl.semaphore_signal(barrier, inc=1, device_id={axis: lax.rem(me + step, n)}, device_id_type=MESH)

    def when(*conditions):
        condition = conditions[0]
        for other in conditions[1:]:
            condition = condition & other
        return pl.when(condition)

    lane = lax.broadcasted_iota(jnp.int32, (extent, LANES), 1)
    live = count[0]

    def turn_probe(s):
        shift = lax.rem(corners[1, s], LANES)
        keep = lane >= shift
        for t in range(2):
            near = pltpu.roll(probe[t, :, 0:LANES], shift, 1)
            far = pltpu.roll(probe[t, :, LANES:], shift, 1)
            zero = jnp.zeros_like(near)
            turned[s, t, :, 0:LANES] = jnp.where(s < live, jnp.where(keep, near, far), zero)
            turned[s, t, :, LANES:] = jnp.where(s < live, jnp.where(keep, far, near), zero)

    def margin_sends(own, right, below, corner, sems, base):
        to_up = [remote(own.at[:, :, r], below.at[:, :, r], sems, base + c, up) for c, r in enumerate(spans)]
        on_up = [remote(right.at[:, :, r], corner.at[:, :, r], sems, base + CHUNKS + c, up) for c, r in enumerate(spans)]
        return to_up, on_up

    def take_below(below, corner, to_up, on_up):
        for c in range(CHUNKS):
            @when(has_down)
            def _():
                to_up[c].wait_recv()
                field[0:2, :, lower[c]] = below[:, :, spans[c]].astype(F32)

            @when(has_down, has_right)
            def _():
                on_up[c].wait_recv()
                field[2:4, :, lower[c]] = corner[:, :, spans[c]].astype(F32)

    def end_up(to_up, on_up):
        @when(has_up)
        def _():
            for copy in to_up:
                copy.wait_send()

        @when(has_up, has_right)
        def _():
            for copy in on_up:
                copy.wait_send()

    def spread():
        own, right, below, corner = tiles0
        sems = (send0, recv0)
        to_up, on_up = margin_sends(own, right, below, corner, sems, 0)
        to_left = [remote(own.at[:, :, r], right.at[:, :, r], sems, 2 * CHUNKS + c, left) for c, r in enumerate(spans)]
        for copy in fetch:
            copy.wait()
        pl.semaphore_wait(barrier, n_y + n_x - 2)
        for c in range(CHUNKS):
            @when(has_left)
            def _():
                to_left[c].start()

            @when(has_up)
            def _():
                to_up[c].start()

        field[0:2, :, 0:tile] = own[...].astype(F32)
        later[0].wait()

        def turn(s, carry):
            turn_probe(s)
            return carry

        lax.fori_loop(0, slots, turn, 0)

        @when(jnp.logical_not(has_right))
        def _():
            field[2:4] = jnp.zeros_like(field[2:4])

        @when(jnp.logical_not(has_down))
        def _():
            field[:, :, tile:] = jnp.zeros_like(field[:, :, tile:])

        for c in range(CHUNKS):
            @when(has_right)
            def _():
                to_left[c].wait_recv()

                @when(has_up)
                def _():
                    on_up[c].start()

                field[2:4, :, spans[c]] = right[:, :, spans[c]].astype(F32)

        def clear(k, carry):
            for t in range(2):
                patches[k, t, 0:tile] = jnp.zeros((tile, LANES), F32)
                patches[k, t, tile + extent:] = jnp.zeros((tile, LANES), F32)
            return carry

        lax.fori_loop(0, 3 * slots, clear, 0)
        patches[3 * slots] = jnp.zeros(patches.shape[1:], F32)
        for copy in later[1:]:
            copy.wait()
        take_below(below, corner, to_up, on_up)

        def end():
            @when(has_left)
            def _():
                for copy in to_left:
                    copy.wait_send()

            end_up(to_up, on_up)

        return end

    def cut(s):
        row, col = corners[0, s], corners[1, s]
        block, shift = col // LANES, lax.rem(col, LANES)
        keep = lane >= shift
        rows = pl.ds(row, extent)
        waves = [[], []]
        for k in range(2):
            halves = []
            for t in range(2):
                if k == 0:
                    halves.append(jnp.where(keep, field[block, t, rows, :], field[block + 2, t, rows, :]))
                else:
                    halves.append(field[block + 1, t, rows, :])
            lanes = slice(k * LANES, (k + 1) * LANES)
            probe_re, probe_im = turned[s, 0, :, lanes], turned[s, 1, :, lanes]
            waves[0].append((probe_re * halves[0] - probe_im * halves[1]).astype(BF16))
            waves[1].append((probe_re * halves[1] + probe_im * halves[0]).astype(BF16))
        return jnp.concatenate(waves[0] + waves[1], 1)

    def put(s, back):
        keep = lane >= lax.rem(corners[1, s], LANES)
        rows = slice(tile, tile + extent)
        for k in range(2):
            lanes = slice(k * LANES, (k + 1) * LANES)
            probe_re, probe_im = turned[s, 0, :, lanes], turned[s, 1, :, lanes]
            re, im = back[:extent, lanes], back[extent:, lanes]
            for t in range(2):
                if t == 0:
                    term = probe_re * re + probe_im * im
                else:
                    term = probe_re * im - probe_im * re
                if k == 0:
                    zero = jnp.zeros_like(term)
                    patches[3 * s, t, rows] = jnp.where(keep, term, zero)
                    patches[3 * s + 2, t, rows] = jnp.where(keep, zero, term)
                else:
                    patches[3 * s + 1, t, rows] = term

    def transform(waves, rhs, lhs):
        half = jnp.dot(waves, rhs[...], preferred_element_type=F32).astype(BF16)
        columns = []
        for g in range(group):
            part = half[g * extent:(g + 1) * extent]
            columns.append(jnp.concatenate([part[:, :extent], part[:, extent:]], 0))
        return jnp.dot(lhs[...], jnp.concatenate(columns, 1), preferred_element_type=F32)

    def sweep(kind, slot_energy):
        def step(index, carry):
            base = index * group
            waves = jnp.concatenate([cut(base + g) for g in range(group)], 0)
            image = transform(waves, table_f, table_g)
            mixed = []
            for g in range(group):
                re = image[:extent, g * extent:(g + 1) * extent]
                im = image[extent:, g * extent:(g + 1) * extent]
                if kind == "first":
                    psi_ref[base + g, 0] = re
                    psi_ref[base + g, 1] = im
                    weight = re * re + im * im - measured[base + g].astype(F32)
                    psi_re, psi_im = re, im
                else:
                    psi_re, psi_im = psi_ref[base + g, 0], psi_ref[base + g, 1]
                    weight = psi_re * re + psi_im * im
                    energy[slot_energy] += jnp.sum((weight * weight).reshape(-1, 8, LANES), 0)
                if kind != "last":
                    mixed.append(jnp.concatenate([(psi_re * weight).astype(BF16), (psi_im * weight).astype(BF16)], 1))
            if kind != "last":
                back = transform(jnp.concatenate(mixed, 0), table_g, table_f)
                for g in range(group):
                    put(base + g, back[:, g * extent:(g + 1) * extent])
            return carry

        lax.fori_loop(0, slots // group, step, 0)

    def gather(start):
        for b in range(4):
            for t in range(2):
                acc = None
                for s in range(slots):
                    row, block = corners[0, s], corners[1, s] // LANES
                    offset = b - block
                    inside = (offset >= 0) & (offset < 3)
                    index = jnp.where(inside, 3 * s + offset, 3 * slots)
                    part = patches[index, t, pl.ds(tile + start - row, size), :]
                    acc = part if acc is None else acc + part
                yield b, t, acc

    def exchange(e, boxes, tiles, sems):
        bottom, inbox_down, side_out, side_in, left_out, left_in = boxes
        own, right, below, corner = tiles
        to_up, on_up = margin_sends(own, right, below, corner, sems, 0)
        to_down = [remote(bottom.at[:, :, r], inbox_down.at[:, :, r], sems, 2 * CHUNKS + c, down) for c, r in enumerate(spans)]
        to_right = [remote(side_out.at[:, :, r], side_in.at[:, :, r], sems, 3 * CHUNKS + c, right_peer) for c, r in enumerate(spans)]
        to_left = [remote(left_out.at[:, :, r], left_in.at[:, :, r], sems, 4 * CHUNKS + c, left) for c, r in enumerate(spans)]

        for c, rows in enumerate(spans):
            for b, t, acc in gather(tile + c * size):
                bottom[b, t, rows] = acc.astype(BF16)

            @when(has_down)
            def _():
                to_down[c].start()

        def send_sideways(c):
            @when(has_right)
            def _():
                side_out[:, :, spans[c]] = total[2:4, :, spans[c]].astype(BF16)
                to_right[c].start()

            @when(has_left)
            def _():
                left_out[:, :, spans[c]] = total[0:2, :, spans[c]].astype(BF16)
                to_left[c].start()

        for c, rows in enumerate(spans):
            for b, t, acc in gather(c * size):
                total[b, t, rows] = acc

            @when(jnp.logical_not(has_up))
            def _():
                send_sideways(c)

        @when(has_up)
        def _():
            for c, rows in enumerate(spans):
                to_down[c].wait_recv()
                total[:, :, rows] += inbox_down[:, :, rows].astype(F32)
                send_sideways(c)

        def scaled(sums, old, rows):
            if e == 0:
                return -2.0 * sums
            return (4.0 * SCALE) * sums + (damping[0] * SCALE) * old[0, :, :, rows]

        for c, rows in enumerate(spans):
            @when(has_left)
            def _():
                to_right[c].wait_recv()
                total[0:2, :, rows] += side_in[:, :, rows].astype(F32)

            value = scaled(total[0:2, :, rows], q, rows)
            q[e, :, :, rows] = value
            own[:, :, rows] = value.astype(BF16)
            field[0:2, :, rows] = own[:, :, rows].astype(F32)

            @when(has_up)
            def _():
                to_up[c].start()

            @when(has_right)
            def _():
                to_left[c].wait_recv()
                value = scaled(total[2:4, :, rows] + left_in[:, :, rows].astype(F32), q_right, rows)
                if e == 0:
                    q_right[e, :, :, rows] = value
                right[:, :, rows] = value.astype(BF16)

                @when(has_up)
                def _():
                    on_up[c].start()

                field[2:4, :, rows] = right[:, :, rows].astype(F32)

        take_below(below, corner, to_up, on_up)

        def end():
            @when(has_down)
            def _():
                for copy in to_down:
                    copy.wait_send()

            @when(has_right)
            def _():
                for copy in to_right:
                    copy.wait_send()

            @when(has_left)
            def _():
                for copy in to_left:
                    copy.wait_send()

            end_up(to_up, on_up)

        return end

    energy[...] = jnp.zeros_like(energy)
    ends = [spread()]
    sweep("first", None)
    ends.append(exchange(0, boxes0, tiles1, (send1, recv1)))
    sweep("middle", 0)
    ends.append(exchange(1, boxes1, tiles2, (send2, recv2)))
    q0, q1 = q[0], q[1]
    rows = [lane_sums(q0 * q0), lane_sums(q1 * q1), lane_sums(energy[0])]
    sweep("last", 1)
    partial = jnp.concatenate(rows + [lane_sums(energy[1]), jnp.zeros((4, LANES), F32)], 0)

    def reduce_over(partial, sums, send, recv, axis, me, n):
        sums[me] = partial
        copies = [
            remote(sums.at[me], sums.at[me], (send, recv), step, {axis: lax.rem(me + step, n)}) for step in range(1, n)
        ]
        for copy in copies:
            copy.start()
        for copy in copies:
            copy.wait()
        return jnp.sum(sums[...], 0)

    partial = reduce_over(partial, sums_y, send_y, recv_y, "ty", ty, n_y)
    partial = reduce_over(partial, sums_x, send_x, recv_x, "tx", tx, n_x)
    dots = jnp.sum(partial, 1, keepdims=True)
    rr, s11, w00, w11 = (dots[k:k + 1] for k in range(4))
    c01 = SCALE * (4.0 * w00 + damping[0] * rr)
    s12 = SCALE * (4.0 * w11 + damping[0] * s11)
    alpha = rr / c01
    rr_next = rr - 2.0 * alpha * c01 + alpha * alpha * s11
    gain = 1.0 + rr_next / rr
    curvature = gain * gain * c01 - 2.0 * gain * alpha * s11 + alpha * alpha * s12
    step_len = rr_next / curvature
    first = (alpha + step_len * gain) * SCALE
    second = step_len * alpha * SCALE
    for h in range(2):
        for t in range(2):
            out_ref[t, :, h * LANES:(h + 1) * LANES] = first * q[0, h, t] - second * q[1, h, t]
    for end in ends:
        end()


def per_device(object_field, probe_field, corners, counts, intensity, damping):
    extent = probe_field.shape[-1]
    tile = object_field.shape[1]
    slots = corners.shape[2]
    group = 4 if slots % 4 == 0 else 1
    n_y, n_x = lax.axis_size("ty"), lax.axis_size("tx")
    places = corners.reshape(slots, 2).T
    measured = intensity.reshape(slots, extent, extent)

    def vmem(shape, dtype):
        return pltpu.VMEM(shape, dtype)

    def sems(n):
        return [pltpu.SemaphoreType.DMA((n,)), pltpu.SemaphoreType.DMA((n,))]

    quarter, whole = (2, 2, tile, LANES), (4, 2, tile, LANES)
    tiles = [vmem(quarter, BF16)] * 4
    boxes = [vmem(whole, BF16)] * 2 + [vmem(quarter, BF16)] * 4
    return pl.pallas_call(
        functools.partial(step_kernel, group, n_y, n_x),
        out_shape=jax.ShapeDtypeStruct((2, tile, tile), F32),
        in_specs=[SMEM_SPEC] * 3 + [ANY_SPEC] * 5,
        out_specs=pl.BlockSpec(memory_space=pltpu.VMEM),
        scratch_shapes=[
            vmem(probe_field.shape, F32),
            vmem(measured.shape, BF16),
            vmem((2 * extent, 2 * extent), BF16),
            vmem((2 * extent, 2 * extent), BF16),
            vmem((slots, 2, extent, extent), F32),
            vmem((slots, 2, extent, extent), F32),
            vmem((4, 2, 2 * tile, LANES), F32),
            vmem((3 * slots + 1, 2, 2 * tile + extent, LANES), F32),
            vmem(whole, F32),
            vmem((2, 8, LANES), F32),
            vmem((2,) + quarter, F32),
            vmem((1,) + quarter, F32),
            tiles, tiles, tiles, boxes, boxes,
            vmem((n_y, 8, LANES), F32),
            vmem((n_x, 8, LANES), F32),
            pltpu.SemaphoreType.DMA((8,)),
        ] + sems(3 * CHUNKS) + sems(5 * CHUNKS) + sems(5 * CHUNKS) + sems(n_y) + sems(n_x),
        compiler_params=pltpu.CompilerParams(collective_id=0, has_side_effects=True, vmem_limit_bytes=58 << 20),
        name="step",
    )(places, counts.reshape(1), damping.reshape(1), object_field, probe_field, measured,
      make_table(extent, -1.0), make_table(extent, 1.0))


def solution(mesh):
    in_specs = (
        P(None, "ty", "tx"),
        P(),
        P("ty", "tx", None, None),
        P("ty", "tx"),
        P("ty", "tx", None, None, None),
        P(),
    )
    out_specs = P(None, "ty", "tx")
    return jax.shard_map(
        per_device, mesh=mesh, in_specs=in_specs, out_specs=out_specs, check_vma=False
    )
```

```python
import functools

import jax
import jax.numpy as jnp
import numpy as np
from jax import lax
from jax.experimental import pallas as pl
from jax.experimental.pallas import tpu as pltpu
from jax.sharding import PartitionSpec as P

MESH = pl.DeviceIdType.MESH
LANES = 128
SCALE = 2.0**-24
CHUNKS = 4
F32 = jnp.float32
BF16 = jnp.bfloat16
SMEM_SPEC = pl.BlockSpec(memory_space=pltpu.SMEM)
ANY_SPEC = pl.BlockSpec(memory_space=pl.ANY)


def make_tables(extent, direction_sign):
    indices = np.arange(extent)
    angles = (indices[:, None] * indices[None, :] % extent) * (2.0 * np.pi / extent)
    cosine = np.cos(angles) / extent**0.5
    sines = direction_sign * np.sin(angles) / extent**0.5
    tables = []
    for parity in range(2):
        re, im = cosine[:extent // 2, parity::2], sines[:extent // 2, parity::2]
        if direction_sign > 0:
            re, im = re.T, im.T
        tables.append(np.block([[re, im], [-im, re]]))
    tables = np.stack(tables + [table.T for table in tables])
    return jnp.asarray(tables.astype(np.float32)).astype(BF16)


def lane_sums(values):
    return jnp.sum(values.reshape(-1, LANES), 0, keepdims=True)


def step_kernel(n_y, n_x, corners, count, damping, object_hbm, probe_hbm, measured_hbm, f_hbm, g_hbm, out_ref,
                probe, measured, table_f, table_g, turned, psi_ref, field, patches, total, energy, q, q_right,
                tiles0, tiles1, tiles2, boxes0, boxes1, sums_y, sums_x,
                local_sem, send0, recv0, send1, recv1, send2, recv2, send_y, recv_y, send_x, recv_x):
    slots, extent, tile = turned.shape[0], probe.shape[-1], total.shape[2]
    half = extent // 2
    ty, tx = lax.axis_index("ty"), lax.axis_index("tx")
    has_up, has_down, has_left, has_right = ty > 0, ty < n_y - 1, tx > 0, tx < n_x - 1
    up, down, left, right_peer = {"ty": ty - 1}, {"ty": ty + 1}, {"tx": tx - 1}, {"tx": tx + 1}
    size = tile // CHUNKS
    spans = [pl.ds(c * size, size) for c in range(CHUNKS)]
    lower = [pl.ds(tile + c * size, size) for c in range(CHUNKS)]

    def remote(src, dst, sems, index, peer):
        return pltpu.make_async_remote_copy(
            src_ref=src, dst_ref=dst, send_sem=sems[0].at[index], recv_sem=sems[1].at[index],
            device_id=peer, device_id_type=MESH,
        )

    own0 = tiles0[0]
    fetch = [
        pltpu.make_async_copy(object_hbm.at[t, :, pl.ds(h * LANES, LANES)], own0.at[h, t], local_sem.at[2 * h + t])
        for h in range(2) for t in range(2)
    ]
    later = [
        pltpu.make_async_copy(src, dst, local_sem.at[4 + k])
        for k, (src, dst) in enumerate(
            ((probe_hbm, probe), (f_hbm, table_f), (g_hbm, table_g), (measured_hbm, measured))
        )
    ]
    for copy in fetch + later:
        copy.start()
    barrier = pltpu.get_barrier_semaphore()
    for axis, me, n in (("ty", ty, n_y), ("tx", tx, n_x)):
        for step in range(1, n):
            pl.semaphore_signal(barrier, inc=1, device_id={axis: lax.rem(me + step, n)}, device_id_type=MESH)

    def when(*conditions):
        condition = conditions[0]
        for other in conditions[1:]:
            condition = condition & other
        return pl.when(condition)

    lane = lax.broadcasted_iota(jnp.int32, (extent, LANES), 1)
    live = count[0]

    def turn_probe(s):
        shift = lax.rem(corners[1, s], LANES)
        keep = lane >= shift
        for t in range(2):
            near = pltpu.roll(probe[t, :, 0:LANES], shift, 1)
            far = pltpu.roll(probe[t, :, LANES:], shift, 1)
            zero = jnp.zeros_like(near)
            turned[s, t, :, 0:LANES] = jnp.where(s < live, jnp.where(keep, near, far), zero)
            turned[s, t, :, LANES:] = jnp.where(s < live, jnp.where(keep, far, near), zero)

    def margin_sends(own, right, below, corner, sems, base):
        to_up = [remote(own.at[:, :, r], below.at[:, :, r], sems, base + c, up) for c, r in enumerate(spans)]
        on_up = [remote(right.at[:, :, r], corner.at[:, :, r], sems, base + CHUNKS + c, up) for c, r in enumerate(spans)]
        return to_up, on_up

    def take_below(below, corner, to_up, on_up):
        for c in range(CHUNKS):
            @when(has_down)
            def _():
                to_up[c].wait_recv()
                field[0:2, :, lower[c]] = below[:, :, spans[c]].astype(F32)

            @when(has_down, has_right)
            def _():
                on_up[c].wait_recv()
                field[2:4, :, lower[c]] = corner[:, :, spans[c]].astype(F32)

    def end_up(to_up, on_up):
        @when(has_up)
        def _():
            for copy in to_up:
                copy.wait_send()

        @when(has_up, has_right)
        def _():
            for copy in on_up:
                copy.wait_send()

    def spread():
        own, right, below, corner = tiles0
        sems = (send0, recv0)
        to_up, on_up = margin_sends(own, right, below, corner, sems, 0)
        to_left = [remote(own.at[:, :, r], right.at[:, :, r], sems, 2 * CHUNKS + c, left) for c, r in enumerate(spans)]
        for copy in fetch:
            copy.wait()
        pl.semaphore_wait(barrier, n_y + n_x - 2)
        for c in range(CHUNKS):
            @when(has_left)
            def _():
                to_left[c].start()

            @when(has_up)
            def _():
                to_up[c].start()

        field[0:2, :, 0:tile] = own[...].astype(F32)
        later[0].wait()

        def turn(s, carry):
            turn_probe(s)
            return carry

        lax.fori_loop(0, slots, turn, 0)
        for copy in later[1:]:
            copy.wait()
        first_index = lax.broadcasted_iota(jnp.int32, (extent, extent), 0)
        second_index = lax.broadcasted_iota(jnp.int32, (extent, extent), 1)
        pick_left = (second_index == 2 * lax.rem(first_index, half) + first_index // half).astype(F32).astype(BF16)
        pick_right = (first_index == 2 * lax.rem(second_index, half) + second_index // half).astype(F32).astype(BF16)

        def reorder(s, carry):
            moved = jnp.dot(measured[s], pick_right, preferred_element_type=F32).astype(BF16)
            measured[s] = jnp.dot(pick_left, moved, preferred_element_type=F32).astype(BF16)
            return carry

        lax.fori_loop(0, slots, reorder, 0)

        @when(jnp.logical_not(has_right))
        def _():
            field[2:4] = jnp.zeros_like(field[2:4])

        @when(jnp.logical_not(has_down))
        def _():
            field[:, :, tile:] = jnp.zeros_like(field[:, :, tile:])

        for c in range(CHUNKS):
            @when(has_right)
            def _():
                to_left[c].wait_recv()

                @when(has_up)
                def _():
                    on_up[c].start()

                field[2:4, :, spans[c]] = right[:, :, spans[c]].astype(F32)

        def clear(k, carry):
            for t in range(2):
                patches[k, t, 0:tile] = jnp.zeros((tile, LANES), F32)
                patches[k, t, tile + extent:] = jnp.zeros((tile, LANES), F32)
            return carry

        lax.fori_loop(0, 3 * slots, clear, 0)
        patches[3 * slots] = jnp.zeros(patches.shape[1:], F32)
        take_below(below, corner, to_up, on_up)

        def end():
            @when(has_left)
            def _():
                for copy in to_left:
                    copy.wait_send()

            end_up(to_up, on_up)

        return end

    def cut(s):
        row, col = corners[0, s], corners[1, s]
        block, shift = col // LANES, lax.rem(col, LANES)
        keep = lane >= shift
        rows = pl.ds(row, extent)
        waves = []
        for k in range(2):
            halves = []
            for t in range(2):
                if k == 0:
                    halves.append(jnp.where(keep, field[block, t, rows, :], field[block + 2, t, rows, :]))
                else:
                    halves.append(field[block + 1, t, rows, :])
            lanes = slice(k * LANES, (k + 1) * LANES)
            probe_re, probe_im = turned[s, 0, :, lanes], turned[s, 1, :, lanes]
            waves.append((probe_re * halves[0] - probe_im * halves[1], probe_re * halves[1] + probe_im * halves[0]))
        (re0, im0), (re1, im1) = waves
        even = jnp.concatenate([(re0 + re1).astype(BF16), (im0 + im1).astype(BF16)], 1)
        odd = jnp.concatenate([(re0 - re1).astype(BF16), (im0 - im1).astype(BF16)], 1)
        return even, odd

    def put(s, back):
        keep = lane >= lax.rem(corners[1, s], LANES)
        rows = slice(tile, tile + extent)
        for k in range(2):
            lanes = slice(k * LANES, (k + 1) * LANES)
            probe_re, probe_im = turned[s, 0, :, lanes], turned[s, 1, :, lanes]
            re, im = back[:extent, lanes], back[extent:, lanes]
            for t in range(2):
                if t == 0:
                    term = probe_re * re + probe_im * im
                else:
                    term = probe_re * im - probe_im * re
                if k == 0:
                    zero = jnp.zeros_like(term)
                    patches[3 * s, t, rows] = jnp.where(keep, term, zero)
                    patches[3 * s + 2, t, rows] = jnp.where(keep, zero, term)
                else:
                    patches[3 * s + 1, t, rows] = term

    def matmul(a, b):
        return jnp.dot(a, b, preferred_element_type=F32)

    def patch_of(s):
        return slice(s * extent, (s + 1) * extent)

    def forward(waves):
        by_column = [matmul(jnp.concatenate([wave[q] for wave in waves], 0), table_f[q]) for q in range(2)]
        operands = [[], []]
        for g in range(len(waves)):
            quarters = [[], []]
            for q in range(2):
                top = by_column[q][g * extent:g * extent + half]
                low = by_column[q][g * extent + half:(g + 1) * extent]
                for p, value in ((0, top + low), (1, top - low)):
                    value = value.astype(BF16)
                    quarters[p].append(jnp.concatenate([value[:, :half], value[:, half:]], 0))
            for p in range(2):
                operands[p].append(jnp.concatenate(quarters[p], 1))
        return [matmul(table_f[2 + p], jnp.concatenate(operands[p], 1)) for p in range(2)]

    def backward(mixed):
        even, odd = (matmul(jnp.concatenate([m[q] for m in mixed], 0), table_g[q]) for q in range(2))
        operands = [[], []]
        for g in range(len(mixed)):
            e, o = even[patch_of(g)], odd[patch_of(g)]
            sides = (e + o).astype(BF16), (e - o).astype(BF16)
            for p in range(2):
                rows = slice(p * half, (p + 1) * half)
                re = jnp.concatenate([side[rows, :half] for side in sides], 1)
                im = jnp.concatenate([side[rows, half:] for side in sides], 1)
                operands[p].append(jnp.concatenate([re, im], 0))
        even, odd = (matmul(table_g[2 + p], jnp.concatenate(operands[p], 1)) for p in range(2))
        backs = []
        for g in range(len(mixed)):
            e, o = even[:, patch_of(g)], odd[:, patch_of(g)]
            top, low = e + o, e - o
            backs.append(jnp.concatenate([top[:half], low[:half], top[half:], low[half:]], 0))
        return backs

    def sweep(kind, slot_energy):
        image = forward([cut(s) for s in range(slots)])
        mixed = []
        for s in range(slots):
            parts = [[], []]
            for p in range(2):
                rows = slice(p * half, (p + 1) * half)
                re, im = image[p][:half, patch_of(s)], image[p][half:, patch_of(s)]
                if kind == "first":
                    psi_ref[s, 0, rows] = re
                    psi_ref[s, 1, rows] = im
                    weight = re * re + im * im - measured[s, rows].astype(F32)
                    psi_re, psi_im = re, im
                else:
                    psi_re, psi_im = psi_ref[s, 0, rows], psi_ref[s, 1, rows]
                    weight = psi_re * re + psi_im * im
                    energy[slot_energy] += jnp.sum((weight * weight).reshape(-1, 8, LANES), 0)
                if kind != "last":
                    pair = (psi_re * weight).astype(BF16), (psi_im * weight).astype(BF16)
                    for q in range(2):
                        parts[q].append(jnp.concatenate([x[:, q * half:(q + 1) * half] for x in pair], 1))
            if kind != "last":
                mixed.append([jnp.concatenate(part, 0) for part in parts])
        if kind != "last":
            for s, back in enumerate(backward(mixed)):
                put(s, back)

    def gather(start):
        for b in range(4):
            for t in range(2):
                acc = None
                for s in range(slots):
                    row, block = corners[0, s], corners[1, s] // LANES
                    offset = b - block
                    inside = (offset >= 0) & (offset < 3)
                    index = jnp.where(inside, 3 * s + offset, 3 * slots)
                    part = patches[index, t, pl.ds(tile + start - row, size), :]
                    acc = part if acc is None else acc + part
                yield b, t, acc

    def exchange(e, boxes, tiles, sems):
        bottom, inbox_down, side_out, side_in, left_out, left_in = boxes
        own, right, below, corner = tiles
        to_up, on_up = margin_sends(own, right, below, corner, sems, 0)
        to_down = [remote(bottom.at[:, :, r], inbox_down.at[:, :, r], sems, 2 * CHUNKS + c, down) for c, r in enumerate(spans)]
        to_right = [remote(side_out.at[:, :, r], side_in.at[:, :, r], sems, 3 * CHUNKS + c, right_peer) for c, r in enumerate(spans)]
        to_left = [remote(left_out.at[:, :, r], left_in.at[:, :, r], sems, 4 * CHUNKS + c, left) for c, r in enumerate(spans)]

        for c, rows in enumerate(spans):
            for b, t, acc in gather(tile + c * size):
                bottom[b, t, rows] = acc.astype(BF16)

            @when(has_down)
            def _():
                to_down[c].start()

        def send_sideways(c):
            @when(has_right)
            def _():
                side_out[:, :, spans[c]] = total[2:4, :, spans[c]].astype(BF16)
                to_right[c].start()

            @when(has_left)
            def _():
                left_out[:, :, spans[c]] = total[0:2, :, spans[c]].astype(BF16)
                to_left[c].start()

        for c, rows in enumerate(spans):
            for b, t, acc in gather(c * size):
                total[b, t, rows] = acc

            @when(jnp.logical_not(has_up))
            def _():
                send_sideways(c)

        @when(has_up)
        def _():
            for c, rows in enumerate(spans):
                to_down[c].wait_recv()
                total[:, :, rows] += inbox_down[:, :, rows].astype(F32)
                send_sideways(c)

        def scaled(sums, old, rows):
            if e == 0:
                return -2.0 * sums
            return (4.0 * SCALE) * sums + (damping[0] * SCALE) * old[0, :, :, rows]

        for c, rows in enumerate(spans):
            @when(has_left)
            def _():
                to_right[c].wait_recv()
                total[0:2, :, rows] += side_in[:, :, rows].astype(F32)

            value = scaled(total[0:2, :, rows], q, rows)
            q[e, :, :, rows] = value
            own[:, :, rows] = value.astype(BF16)
            field[0:2, :, rows] = own[:, :, rows].astype(F32)

            @when(has_up)
            def _():
                to_up[c].start()

            @when(has_right)
            def _():
                to_left[c].wait_recv()
                value = scaled(total[2:4, :, rows] + left_in[:, :, rows].astype(F32), q_right, rows)
                if e == 0:
                    q_right[e, :, :, rows] = value
                right[:, :, rows] = value.astype(BF16)

                @when(has_up)
                def _():
                    on_up[c].start()

                field[2:4, :, rows] = right[:, :, rows].astype(F32)

        take_below(below, corner, to_up, on_up)

        def end():
            @when(has_down)
            def _():
                for copy in to_down:
                    copy.wait_send()

            @when(has_right)
            def _():
                for copy in to_right:
                    copy.wait_send()

            @when(has_left)
            def _():
                for copy in to_left:
                    copy.wait_send()

            end_up(to_up, on_up)

        return end

    energy[...] = jnp.zeros_like(energy)
    ends = [spread()]
    sweep("first", None)
    ends.append(exchange(0, boxes0, tiles1, (send1, recv1)))
    sweep("middle", 0)
    ends.append(exchange(1, boxes1, tiles2, (send2, recv2)))
    q0, q1 = q[0], q[1]
    rows = [lane_sums(q0 * q0), lane_sums(q1 * q1), lane_sums(energy[0])]
    sweep("last", 1)
    partial = jnp.concatenate(rows + [lane_sums(energy[1]), jnp.zeros((4, LANES), F32)], 0)

    def reduce_over(partial, sums, send, recv, axis, me, n):
        sums[me] = partial
        copies = [
            remote(sums.at[me], sums.at[me], (send, recv), step, {axis: lax.rem(me + step, n)}) for step in range(1, n)
        ]
        for copy in copies:
            copy.start()
        for copy in copies:
            copy.wait()
        return jnp.sum(sums[...], 0)

    partial = reduce_over(partial, sums_y, send_y, recv_y, "ty", ty, n_y)
    partial = reduce_over(partial, sums_x, send_x, recv_x, "tx", tx, n_x)
    dots = jnp.sum(partial, 1, keepdims=True)
    rr, s11, w00, w11 = (dots[k:k + 1] for k in range(4))
    c01 = SCALE * (4.0 * w00 + damping[0] * rr)
    s12 = SCALE * (4.0 * w11 + damping[0] * s11)
    alpha = rr / c01
    rr_next = rr - 2.0 * alpha * c01 + alpha * alpha * s11
    gain = 1.0 + rr_next / rr
    curvature = gain * gain * c01 - 2.0 * gain * alpha * s11 + alpha * alpha * s12
    step_len = rr_next / curvature
    first = (alpha + step_len * gain) * SCALE
    second = step_len * alpha * SCALE
    for h in range(2):
        for t in range(2):
            out_ref[t, :, h * LANES:(h + 1) * LANES] = first * q[0, h, t] - second * q[1, h, t]
    for end in ends:
        end()


def per_device(object_field, probe_field, corners, counts, intensity, damping):
    extent = probe_field.shape[-1]
    tile = object_field.shape[1]
    slots = corners.shape[2]
    n_y, n_x = lax.axis_size("ty"), lax.axis_size("tx")
    places = corners.reshape(slots, 2).T
    measured = intensity.reshape(slots, extent, extent)

    def vmem(shape, dtype):
        return pltpu.VMEM(shape, dtype)

    def sems(n):
        return [pltpu.SemaphoreType.DMA((n,)), pltpu.SemaphoreType.DMA((n,))]

    quarter, whole = (2, 2, tile, LANES), (4, 2, tile, LANES)
    tiles = [vmem(quarter, BF16)] * 4
    boxes = [vmem(whole, BF16)] * 2 + [vmem(quarter, BF16)] * 4
    return pl.pallas_call(
        functools.partial(step_kernel, n_y, n_x),
        out_shape=jax.ShapeDtypeStruct((2, tile, tile), F32),
        in_specs=[SMEM_SPEC] * 3 + [ANY_SPEC] * 5,
        out_specs=pl.BlockSpec(memory_space=pltpu.VMEM),
        scratch_shapes=[
            vmem(probe_field.shape, F32),
            vmem(measured.shape, BF16),
            vmem((4, extent, extent), BF16),
            vmem((4, extent, extent), BF16),
            vmem((slots, 2, extent, extent), F32),
            vmem((slots, 2, extent, extent), F32),
            vmem((4, 2, 2 * tile, LANES), F32),
            vmem((3 * slots + 1, 2, 2 * tile + extent, LANES), F32),
            vmem(whole, F32),
            vmem((2, 8, LANES), F32),
            vmem((2,) + quarter, F32),
            vmem((1,) + quarter, F32),
            tiles, tiles, tiles, boxes, boxes,
            vmem((n_y, 8, LANES), F32),
            vmem((n_x, 8, LANES), F32),
            pltpu.SemaphoreType.DMA((8,)),
        ] + sems(3 * CHUNKS) + sems(5 * CHUNKS) + sems(5 * CHUNKS) + sems(n_y) + sems(n_x),
        compiler_params=pltpu.CompilerParams(collective_id=0, has_side_effects=True, vmem_limit_bytes=58 << 20),
        name="step",
    )(places, counts.reshape(1), damping.reshape(1), object_field, probe_field, measured,
      make_tables(extent, -1.0), make_tables(extent, 1.0))


def solution(mesh):
    in_specs = (
        P(None, "ty", "tx"),
        P(),
        P("ty", "tx", None, None),
        P("ty", "tx"),
        P("ty", "tx", None, None, None),
        P(),
    )
    out_specs = P(None, "ty", "tx")
    return jax.shard_map(
        per_device, mesh=mesh, in_specs=in_specs, out_specs=out_specs, check_vma=False
    )
```

```python
import functools

import jax
import jax.numpy as jnp
import numpy as np
from jax import lax
from jax.experimental import pallas as pl
from jax.experimental.pallas import tpu as pltpu
from jax.sharding import PartitionSpec as P

MESH = pl.DeviceIdType.MESH
LANES = 128
SCALE = 2.0**-24
CHUNKS = 4
F32 = jnp.float32
BF16 = jnp.bfloat16
SMEM_SPEC = pl.BlockSpec(memory_space=pltpu.SMEM)
ANY_SPEC = pl.BlockSpec(memory_space=pl.ANY)


def make_tables(extent, direction_sign):
    indices = np.arange(extent)
    angles = (indices[:, None] * indices[None, :] % extent) * (2.0 * np.pi / extent)
    cosine = np.cos(angles) / extent**0.5
    sines = direction_sign * np.sin(angles) / extent**0.5
    tables = []
    for parity in range(2):
        re, im = cosine[:extent // 2, parity::2], sines[:extent // 2, parity::2]
        if direction_sign > 0:
            re, im = re.T, im.T
        tables.append(np.block([[re, im], [-im, re]]))
    tables = np.stack(tables + [table.T for table in tables])
    return jnp.asarray(tables.astype(np.float32)).astype(BF16)


def lane_sums(values):
    return jnp.sum(values.reshape(-1, LANES), 0, keepdims=True)


def step_kernel(n_y, n_x, corners, count, damping, object_hbm, probe_hbm, measured_hbm, f_hbm, g_hbm, out_ref,
                probe, measured, table_f, table_g, turned, psi_ref, field, patches, total, energy, q, q_right,
                tiles0, tiles1, tiles2, boxes0, boxes1, sums_y, sums_x,
                local_sem, send0, recv0, send1, recv1, send2, recv2, send_y, recv_y, send_x, recv_x):
    slots, extent, tile = turned.shape[0], probe.shape[-1], total.shape[2]
    half = extent // 2
    ty, tx = lax.axis_index("ty"), lax.axis_index("tx")
    has_up, has_down, has_left, has_right = ty > 0, ty < n_y - 1, tx > 0, tx < n_x - 1
    up, down, left, right_peer = {"ty": ty - 1}, {"ty": ty + 1}, {"tx": tx - 1}, {"tx": tx + 1}
    size = tile // CHUNKS
    spans = [pl.ds(c * size, size) for c in range(CHUNKS)]
    lower = [pl.ds(tile + c * size, size) for c in range(CHUNKS)]

    def remote(src, dst, sems, index, peer):
        return pltpu.make_async_remote_copy(
            src_ref=src, dst_ref=dst, send_sem=sems[0].at[index], recv_sem=sems[1].at[index],
            device_id=peer, device_id_type=MESH,
        )

    own0 = tiles0[0]
    fetch = [
        pltpu.make_async_copy(object_hbm.at[t, :, pl.ds(h * LANES, LANES)], own0.at[h, t], local_sem.at[2 * h + t])
        for h in range(2) for t in range(2)
    ]
    later = [
        pltpu.make_async_copy(src, dst, local_sem.at[4 + k])
        for k, (src, dst) in enumerate(
            ((probe_hbm, probe), (f_hbm, table_f), (g_hbm, table_g), (measured_hbm, measured))
        )
    ]
    for copy in fetch + later:
        copy.start()
    barrier = pltpu.get_barrier_semaphore()
    for axis, me, n in (("ty", ty, n_y), ("tx", tx, n_x)):
        for step in range(1, n):
            pl.semaphore_signal(barrier, inc=1, device_id={axis: lax.rem(me + step, n)}, device_id_type=MESH)

    def when(*conditions):
        condition = conditions[0]
        for other in conditions[1:]:
            condition = condition & other
        return pl.when(condition)

    lane = lax.broadcasted_iota(jnp.int32, (extent, LANES), 1)
    live = count[0]

    def turn_probe(s):
        shift = lax.rem(corners[1, s], LANES)
        keep = lane >= shift
        for t in range(2):
            near = pltpu.roll(probe[t, :, 0:LANES], shift, 1)
            far = pltpu.roll(probe[t, :, LANES:], shift, 1)
            zero = jnp.zeros_like(near)
            turned[s, t, :, 0:LANES] = jnp.where(s < live, jnp.where(keep, near, far), zero)
            turned[s, t, :, LANES:] = jnp.where(s < live, jnp.where(keep, far, near), zero)

    def margin_sends(own, right, below, corner, sems, base):
        to_up = [remote(own.at[:, :, r], below.at[:, :, r], sems, base + c, up) for c, r in enumerate(spans)]
        on_up = [remote(right.at[:, :, r], corner.at[:, :, r], sems, base + CHUNKS + c, up) for c, r in enumerate(spans)]
        return to_up, on_up

    def take_below(below, corner, to_up, on_up):
        for c in range(CHUNKS):
            @when(has_down)
            def _():
                to_up[c].wait_recv()
                field[0:2, :, lower[c]] = below[:, :, spans[c]].astype(F32)

            @when(has_down, has_right)
            def _():
                on_up[c].wait_recv()
                field[2:4, :, lower[c]] = corner[:, :, spans[c]].astype(F32)

    def end_up(to_up, on_up):
        @when(has_up)
        def _():
            for copy in to_up:
                copy.wait_send()

        @when(has_up, has_right)
        def _():
            for copy in on_up:
                copy.wait_send()

    def spread():
        own, right, below, corner = tiles0
        sems = (send0, recv0)
        to_up, on_up = margin_sends(own, right, below, corner, sems, 0)
        to_left = [remote(own.at[:, :, r], right.at[:, :, r], sems, 2 * CHUNKS + c, left) for c, r in enumerate(spans)]
        for copy in fetch:
            copy.wait()
        pl.semaphore_wait(barrier, n_y + n_x - 2)
        for c in range(CHUNKS):
            @when(has_left)
            def _():
                to_left[c].start()

            @when(has_up)
            def _():
                to_up[c].start()

        field[0:2, :, 0:tile] = own[...].astype(F32)
        later[0].wait()

        def turn(s, carry):
            turn_probe(s)
            return carry

        lax.fori_loop(0, slots, turn, 0)
        for copy in later[1:]:
            copy.wait()
        def clear(k, carry):
            for t in range(2):
                patches[k, t, 0:tile] = jnp.zeros((tile, LANES), F32)
                patches[k, t, tile + extent:] = jnp.zeros((tile, LANES), F32)
            return carry

        lax.fori_loop(0, 3 * slots, clear, 0)
        patches[3 * slots] = jnp.zeros(patches.shape[1:], F32)
        @when(jnp.logical_not(has_right))
        def _():
            field[2:4] = jnp.zeros_like(field[2:4])

        @when(jnp.logical_not(has_down))
        def _():
            field[:, :, tile:] = jnp.zeros_like(field[:, :, tile:])

        for c in range(CHUNKS):
            @when(has_right)
            def _():
                to_left[c].wait_recv()

                @when(has_up)
                def _():
                    on_up[c].start()

                field[2:4, :, spans[c]] = right[:, :, spans[c]].astype(F32)

        first_index = lax.broadcasted_iota(jnp.int32, (extent, extent), 0)
        second_index = lax.broadcasted_iota(jnp.int32, (extent, extent), 1)
        pick_left = (second_index == 2 * lax.rem(first_index, half) + first_index // half).astype(F32).astype(BF16)
        pick_right = (first_index == 2 * lax.rem(second_index, half) + second_index // half).astype(F32).astype(BF16)

        def reorder(s, carry):
            moved = jnp.dot(measured[s], pick_right, preferred_element_type=F32).astype(BF16)
            measured[s] = jnp.dot(pick_left, moved, preferred_element_type=F32).astype(BF16)
            return carry

        lax.fori_loop(0, slots, reorder, 0)

        take_below(below, corner, to_up, on_up)

        def end():
            @when(has_left)
            def _():
                for copy in to_left:
                    copy.wait_send()

            end_up(to_up, on_up)

        return end

    def cut(s):
        row, col = corners[0, s], corners[1, s]
        block, shift = col // LANES, lax.rem(col, LANES)
        keep = lane >= shift
        rows = pl.ds(row, extent)
        waves = []
        for k in range(2):
            halves = []
            for t in range(2):
                if k == 0:
                    halves.append(jnp.where(keep, field[block, t, rows, :], field[block + 2, t, rows, :]))
                else:
                    halves.append(field[block + 1, t, rows, :])
            lanes = slice(k * LANES, (k + 1) * LANES)
            probe_re, probe_im = turned[s, 0, :, lanes], turned[s, 1, :, lanes]
            waves.append((probe_re * halves[0] - probe_im * halves[1], probe_re * halves[1] + probe_im * halves[0]))
        (re0, im0), (re1, im1) = waves
        even = jnp.concatenate([(re0 + re1).astype(BF16), (im0 + im1).astype(BF16)], 1)
        odd = jnp.concatenate([(re0 - re1).astype(BF16), (im0 - im1).astype(BF16)], 1)
        return even, odd

    def put(s, back):
        keep = lane >= lax.rem(corners[1, s], LANES)
        rows = slice(tile, tile + extent)
        for k in range(2):
            lanes = slice(k * LANES, (k + 1) * LANES)
            probe_re, probe_im = turned[s, 0, :, lanes], turned[s, 1, :, lanes]
            re, im = back[:extent, lanes], back[extent:, lanes]
            for t in range(2):
                if t == 0:
                    term = probe_re * re + probe_im * im
                else:
                    term = probe_re * im - probe_im * re
                if k == 0:
                    zero = jnp.zeros_like(term)
                    patches[3 * s, t, rows] = jnp.where(keep, term, zero)
                    patches[3 * s + 2, t, rows] = jnp.where(keep, zero, term)
                else:
                    patches[3 * s + 1, t, rows] = term

    def matmul(a, b):
        return jnp.dot(a, b, preferred_element_type=F32)

    def patch_of(s):
        return slice(s * extent, (s + 1) * extent)

    def forward(waves):
        by_column = [matmul(jnp.concatenate([wave[q] for wave in waves], 0), table_f[q]).astype(BF16) for q in range(2)]
        operands = [[], []]
        for g in range(len(waves)):
            quarters = [[], []]
            for q in range(2):
                top = by_column[q][g * extent:g * extent + half]
                low = by_column[q][g * extent + half:(g + 1) * extent]
                for p, value in ((0, top + low), (1, top - low)):
                    quarters[p].append(jnp.concatenate([value[:, :half], value[:, half:]], 0))
            for p in range(2):
                operands[p].append(jnp.concatenate(quarters[p], 1))
        return [matmul(table_f[2 + p], jnp.concatenate(operands[p], 1)) for p in range(2)]

    def backward(mixed):
        even, odd = (matmul(jnp.concatenate([m[q] for m in mixed], 0), table_g[q]).astype(BF16) for q in range(2))
        operands = [[], []]
        for g in range(len(mixed)):
            e, o = even[patch_of(g)], odd[patch_of(g)]
            sides = e + o, e - o
            for p in range(2):
                rows = slice(p * half, (p + 1) * half)
                re = jnp.concatenate([side[rows, :half] for side in sides], 1)
                im = jnp.concatenate([side[rows, half:] for side in sides], 1)
                operands[p].append(jnp.concatenate([re, im], 0))
        even, odd = (matmul(table_g[2 + p], jnp.concatenate(operands[p], 1)) for p in range(2))
        backs = []
        for g in range(len(mixed)):
            e, o = even[:, patch_of(g)], odd[:, patch_of(g)]
            top, low = e + o, e - o
            backs.append(jnp.concatenate([top[:half], low[:half], top[half:], low[half:]], 0))
        return backs

    def sweep(kind, slot_energy):
        image = forward([cut(s) for s in range(slots)])
        mixed, squares = [], None
        for s in range(slots):
            parts = [[], []]
            for p in range(2):
                rows = slice(p * half, (p + 1) * half)
                re, im = image[p][:half, patch_of(s)], image[p][half:, patch_of(s)]
                if kind == "first":
                    psi_ref[s, 0, rows] = re
                    psi_ref[s, 1, rows] = im
                    weight = re * re + im * im - measured[s, rows].astype(F32)
                    psi_re, psi_im = re, im
                else:
                    psi_re, psi_im = psi_ref[s, 0, rows], psi_ref[s, 1, rows]
                    weight = psi_re * re + psi_im * im
                    square = weight * weight
                    square = jnp.sum((square[:, :half] + square[:, half:]).reshape(-1, 8, half), 0)
                    squares = square if squares is None else squares + square
                if kind != "last":
                    pair = (psi_re * weight).astype(BF16), (psi_im * weight).astype(BF16)
                    for q in range(2):
                        parts[q].append(jnp.concatenate([x[:, q * half:(q + 1) * half] for x in pair], 1))
            if kind != "last":
                mixed.append([jnp.concatenate(part, 0) for part in parts])
        if kind != "first":
            energy[slot_energy] = squares
        if kind != "last":
            for s, back in enumerate(backward(mixed)):
                put(s, back)

    def gather(start):
        for b in range(4):
            for t in range(2):
                acc = None
                for s in range(slots):
                    row, block = corners[0, s], corners[1, s] // LANES
                    offset = b - block
                    inside = (offset >= 0) & (offset < 3)
                    index = jnp.where(inside, 3 * s + offset, 3 * slots)
                    part = patches[index, t, pl.ds(tile + start - row, size), :]
                    acc = part if acc is None else acc + part
                yield b, t, acc

    def exchange(e, boxes, tiles, sems):
        bottom, inbox_down, side_out, side_in, left_out, left_in = boxes
        own, right, below, corner = tiles
        to_up, on_up = margin_sends(own, right, below, corner, sems, 0)
        to_down = [remote(bottom.at[:, :, r], inbox_down.at[:, :, r], sems, 2 * CHUNKS + c, down) for c, r in enumerate(spans)]
        to_right = [remote(side_out.at[:, :, r], side_in.at[:, :, r], sems, 3 * CHUNKS + c, right_peer) for c, r in enumerate(spans)]
        to_left = [remote(left_out.at[:, :, r], left_in.at[:, :, r], sems, 4 * CHUNKS + c, left) for c, r in enumerate(spans)]

        for c, rows in enumerate(spans):
            for b, t, acc in gather(tile + c * size):
                bottom[b, t, rows] = acc.astype(BF16)

            @when(has_down)
            def _():
                to_down[c].start()

        def send_sideways(c):
            @when(has_right)
            def _():
                side_out[:, :, spans[c]] = total[2:4, :, spans[c]].astype(BF16)
                to_right[c].start()

            @when(has_left)
            def _():
                left_out[:, :, spans[c]] = total[0:2, :, spans[c]].astype(BF16)
                to_left[c].start()

        for c, rows in enumerate(spans):
            for b, t, acc in gather(c * size):
                total[b, t, rows] = acc

            @when(jnp.logical_not(has_up))
            def _():
                send_sideways(c)

        @when(has_up)
        def _():
            for c, rows in enumerate(spans):
                to_down[c].wait_recv()
                total[:, :, rows] += inbox_down[:, :, rows].astype(F32)
                send_sideways(c)

        def scaled(sums, old, rows):
            if e == 0:
                return -2.0 * sums
            return (4.0 * SCALE) * sums + (damping[0] * SCALE) * old[0, :, :, rows]

        for c, rows in enumerate(spans):
            @when(has_left)
            def _():
                to_right[c].wait_recv()
                total[0:2, :, rows] += side_in[:, :, rows].astype(F32)

            value = scaled(total[0:2, :, rows], q, rows)
            q[e, :, :, rows] = value
            own[:, :, rows] = value.astype(BF16)
            field[0:2, :, rows] = own[:, :, rows].astype(F32)

            @when(has_up)
            def _():
                to_up[c].start()

            @when(has_right)
            def _():
                to_left[c].wait_recv()
                value = scaled(total[2:4, :, rows] + left_in[:, :, rows].astype(F32), q_right, rows)
                if e == 0:
                    q_right[e, :, :, rows] = value
                right[:, :, rows] = value.astype(BF16)

                @when(has_up)
                def _():
                    on_up[c].start()

                field[2:4, :, rows] = right[:, :, rows].astype(F32)

        take_below(below, corner, to_up, on_up)

        def end():
            @when(has_down)
            def _():
                for copy in to_down:
                    copy.wait_send()

            @when(has_right)
            def _():
                for copy in to_right:
                    copy.wait_send()

            @when(has_left)
            def _():
                for copy in to_left:
                    copy.wait_send()

            end_up(to_up, on_up)

        return end

    ends = [spread()]
    sweep("first", None)
    ends.append(exchange(0, boxes0, tiles1, (send1, recv1)))
    sweep("middle", 0)
    ends.append(exchange(1, boxes1, tiles2, (send2, recv2)))
    q0, q1 = q[0], q[1]
    rows = [lane_sums(q0 * q0), lane_sums(q1 * q1), lane_sums(energy[0])]
    sweep("last", 1)
    partial = jnp.concatenate(rows + [lane_sums(energy[1]), jnp.zeros((4, LANES), F32)], 0)

    def reduce_over(partial, sums, send, recv, axis, me, n):
        sums[me] = partial
        copies = [
            remote(sums.at[me], sums.at[me], (send, recv), step, {axis: lax.rem(me + step, n)}) for step in range(1, n)
        ]
        for copy in copies:
            copy.start()
        for copy in copies:
            copy.wait()
        return jnp.sum(sums[...], 0)

    partial = reduce_over(partial, sums_y, send_y, recv_y, "ty", ty, n_y)
    partial = reduce_over(partial, sums_x, send_x, recv_x, "tx", tx, n_x)
    dots = jnp.sum(partial, 1, keepdims=True)
    rr, s11, w00, w11 = (dots[k:k + 1] for k in range(4))
    c01 = SCALE * (4.0 * w00 + damping[0] * rr)
    s12 = SCALE * (4.0 * w11 + damping[0] * s11)
    alpha = rr / c01
    rr_next = rr - 2.0 * alpha * c01 + alpha * alpha * s11
    gain = 1.0 + rr_next / rr
    curvature = gain * gain * c01 - 2.0 * gain * alpha * s11 + alpha * alpha * s12
    step_len = rr_next / curvature
    first = (alpha + step_len * gain) * SCALE
    second = step_len * alpha * SCALE
    for h in range(2):
        for t in range(2):
            out_ref[t, :, h * LANES:(h + 1) * LANES] = first * q[0, h, t] - second * q[1, h, t]
    for end in ends:
        end()


def per_device(object_field, probe_field, corners, counts, intensity, damping):
    extent = probe_field.shape[-1]
    tile = object_field.shape[1]
    slots = corners.shape[2]
    n_y, n_x = lax.axis_size("ty"), lax.axis_size("tx")
    places = corners.reshape(slots, 2).T
    measured = intensity.reshape(slots, extent, extent)

    def vmem(shape, dtype):
        return pltpu.VMEM(shape, dtype)

    def sems(n):
        return [pltpu.SemaphoreType.DMA((n,)), pltpu.SemaphoreType.DMA((n,))]

    quarter, whole = (2, 2, tile, LANES), (4, 2, tile, LANES)
    tiles = [vmem(quarter, BF16)] * 4
    boxes = [vmem(whole, BF16)] * 2 + [vmem(quarter, BF16)] * 4
    return pl.pallas_call(
        functools.partial(step_kernel, n_y, n_x),
        out_shape=jax.ShapeDtypeStruct((2, tile, tile), F32),
        in_specs=[SMEM_SPEC] * 3 + [ANY_SPEC] * 5,
        out_specs=pl.BlockSpec(memory_space=pltpu.VMEM),
        scratch_shapes=[
            vmem(probe_field.shape, F32),
            vmem(measured.shape, BF16),
            vmem((4, extent, extent), BF16),
            vmem((4, extent, extent), BF16),
            vmem((slots, 2, extent, extent), F32),
            vmem((slots, 2, extent, extent), F32),
            vmem((4, 2, 2 * tile, LANES), F32),
            vmem((3 * slots + 1, 2, 2 * tile + extent, LANES), F32),
            vmem(whole, F32),
            vmem((2, 8, LANES), F32),
            vmem((2,) + quarter, F32),
            vmem((1,) + quarter, F32),
            tiles, tiles, tiles, boxes, boxes,
            vmem((n_y, 8, LANES), F32),
            vmem((n_x, 8, LANES), F32),
            pltpu.SemaphoreType.DMA((8,)),
        ] + sems(3 * CHUNKS) + sems(5 * CHUNKS) + sems(5 * CHUNKS) + sems(n_y) + sems(n_x),
        compiler_params=pltpu.CompilerParams(collective_id=0, has_side_effects=True, vmem_limit_bytes=58 << 20),
        name="step",
    )(places, counts.reshape(1), damping.reshape(1), object_field, probe_field, measured,
      make_tables(extent, -1.0), make_tables(extent, 1.0))


def solution(mesh):
    in_specs = (
        P(None, "ty", "tx"),
        P(),
        P("ty", "tx", None, None),
        P("ty", "tx"),
        P("ty", "tx", None, None, None),
        P(),
    )
    out_specs = P(None, "ty", "tx")
    return jax.shard_map(
        per_device, mesh=mesh, in_specs=in_specs, out_specs=out_specs, check_vma=False
    )
```

```python
import functools

import jax
import jax.numpy as jnp
import numpy as np
from jax import lax
from jax.experimental import pallas as pl
from jax.experimental.pallas import tpu as pltpu
from jax.sharding import PartitionSpec as P

MESH = pl.DeviceIdType.MESH
LANES = 128
SCALE = 2.0**-24
CHUNKS = 4
F32 = jnp.float32
BF16 = jnp.bfloat16
SMEM_SPEC = pl.BlockSpec(memory_space=pltpu.SMEM)
ANY_SPEC = pl.BlockSpec(memory_space=pl.ANY)


def make_tables(extent, direction_sign):
    indices = np.arange(extent)
    angles = (indices[:, None] * indices[None, :] % extent) * (2.0 * np.pi / extent)
    cosine = np.cos(angles) / extent**0.5
    sines = direction_sign * np.sin(angles) / extent**0.5
    tables = []
    for parity in range(2):
        re, im = cosine[:extent // 2, parity::2], sines[:extent // 2, parity::2]
        if direction_sign > 0:
            re, im = re.T, im.T
        tables.append(np.block([[re, im], [-im, re]]))
    tables = np.stack(tables + [table.T for table in tables])
    return jnp.asarray(tables.astype(np.float32)).astype(BF16)


def lane_sums(values):
    return jnp.sum(values.reshape(-1, LANES), 0, keepdims=True)


def step_kernel(n_y, n_x, corners, count, damping, object_hbm, probe_hbm, measured_hbm, f_hbm, g_hbm, out_ref,
                probe, measured, table_f, table_g, turned, psi_ref, field, patches, total, energy, q, q_right,
                tiles0, tiles1, tiles2, boxes0, boxes1, sums_y, sums_x,
                local_sem, send0, recv0, send1, recv1, send2, recv2, send_y, recv_y, send_x, recv_x):
    slots, extent, tile = turned.shape[0], probe.shape[-1], total.shape[2]
    half = extent // 2
    ty, tx = lax.axis_index("ty"), lax.axis_index("tx")
    has_up, has_down, has_left, has_right = ty > 0, ty < n_y - 1, tx > 0, tx < n_x - 1
    up, down, left, right_peer = {"ty": ty - 1}, {"ty": ty + 1}, {"tx": tx - 1}, {"tx": tx + 1}
    size = tile // CHUNKS
    spans = [pl.ds(c * size, size) for c in range(CHUNKS)]
    lower = [pl.ds(tile + c * size, size) for c in range(CHUNKS)]

    def remote(src, dst, sems, index, peer):
        return pltpu.make_async_remote_copy(
            src_ref=src, dst_ref=dst, send_sem=sems[0].at[index], recv_sem=sems[1].at[index],
            device_id=peer, device_id_type=MESH,
        )

    own0 = tiles0[0]
    fetch = [
        pltpu.make_async_copy(object_hbm.at[t, :, pl.ds(h * LANES, LANES)], own0.at[h, t], local_sem.at[2 * h + t])
        for h in range(2) for t in range(2)
    ]
    later = [
        pltpu.make_async_copy(src, dst, local_sem.at[4 + k])
        for k, (src, dst) in enumerate(
            ((probe_hbm, probe), (f_hbm, table_f), (g_hbm, table_g), (measured_hbm, measured))
        )
    ]
    for copy in fetch + later:
        copy.start()
    barrier = pltpu.get_barrier_semaphore()
    for axis, me, n in (("ty", ty, n_y), ("tx", tx, n_x)):
        for step in range(1, n):
            pl.semaphore_signal(barrier, inc=1, device_id={axis: lax.rem(me + step, n)}, device_id_type=MESH)

    def when(*conditions):
        condition = conditions[0]
        for other in conditions[1:]:
            condition = condition & other
        return pl.when(condition)

    lane = lax.broadcasted_iota(jnp.int32, (extent, LANES), 1)
    live = count[0]

    def turn_probe(s):
        shift = lax.rem(corners[1, s], LANES)
        keep = lane >= shift
        for t in range(2):
            near = pltpu.roll(probe[t, :, 0:LANES], shift, 1)
            far = pltpu.roll(probe[t, :, LANES:], shift, 1)
            zero = jnp.zeros_like(near)
            turned[s, t, :, 0:LANES] = jnp.where(s < live, jnp.where(keep, near, far), zero)
            turned[s, t, :, LANES:] = jnp.where(s < live, jnp.where(keep, far, near), zero)

    def margin_sends(own, right, below, corner, sems, base):
        to_up = [remote(own.at[:, :, r], below.at[:, :, r], sems, base + c, up) for c, r in enumerate(spans)]
        on_up = [remote(right.at[:, :, r], corner.at[:, :, r], sems, base + CHUNKS + c, up) for c, r in enumerate(spans)]
        return to_up, on_up

    def take_below(below, corner, to_up, on_up):
        for c in range(CHUNKS):
            @when(has_down)
            def _():
                to_up[c].wait_recv()
                field[0:2, :, lower[c]] = below[:, :, spans[c]].astype(F32)

            @when(has_down, has_right)
            def _():
                on_up[c].wait_recv()
                field[2:4, :, lower[c]] = corner[:, :, spans[c]].astype(F32)

    def end_up(to_up, on_up):
        @when(has_up)
        def _():
            for copy in to_up:
                copy.wait_send()

        @when(has_up, has_right)
        def _():
            for copy in on_up:
                copy.wait_send()

    def spread():
        own, right, below, corner = tiles0
        sems = (send0, recv0)
        to_up, on_up = margin_sends(own, right, below, corner, sems, 0)
        to_left = [remote(own.at[:, :, r], right.at[:, :, r], sems, 2 * CHUNKS + c, left) for c, r in enumerate(spans)]
        for copy in fetch:
            copy.wait()
        pl.semaphore_wait(barrier, n_y + n_x - 2)
        for c in range(CHUNKS):
            @when(has_left)
            def _():
                to_left[c].start()

            @when(has_up)
            def _():
                to_up[c].start()

        field[0:2, :, 0:tile] = own[...].astype(F32)
        later[0].wait()

        def turn(s, carry):
            turn_probe(s)
            return carry

        lax.fori_loop(0, slots, turn, 0)
        for copy in later[1:]:
            copy.wait()
        first_index = lax.broadcasted_iota(jnp.int32, (extent, extent), 0)
        second_index = lax.broadcasted_iota(jnp.int32, (extent, extent), 1)
        pick_left = (second_index == 2 * lax.rem(first_index, half) + first_index // half).astype(F32).astype(BF16)
        pick_right = (first_index == 2 * lax.rem(second_index, half) + second_index // half).astype(F32).astype(BF16)

        def reorder(s, carry):
            moved = jnp.dot(measured[s], pick_right, preferred_element_type=F32).astype(BF16)
            measured[s] = jnp.dot(pick_left, moved, preferred_element_type=F32).astype(BF16)
            return carry

        lax.fori_loop(0, slots, reorder, 0)

        @when(jnp.logical_not(has_right))
        def _():
            field[2:4] = jnp.zeros_like(field[2:4])

        @when(jnp.logical_not(has_down))
        def _():
            field[:, :, tile:] = jnp.zeros_like(field[:, :, tile:])

        for c in range(CHUNKS):
            @when(has_right)
            def _():
                to_left[c].wait_recv()

                @when(has_up)
                def _():
                    on_up[c].start()

                field[2:4, :, spans[c]] = right[:, :, spans[c]].astype(F32)

        def clear(k, carry):
            for t in range(2):
                patches[k, t, 0:tile] = jnp.zeros((tile, LANES), F32)
                patches[k, t, tile + extent:] = jnp.zeros((tile, LANES), F32)
            return carry

        lax.fori_loop(0, 3 * slots, clear, 0)
        patches[3 * slots] = jnp.zeros(patches.shape[1:], F32)
        take_below(below, corner, to_up, on_up)

        def end():
            @when(has_left)
            def _():
                for copy in to_left:
                    copy.wait_send()

            end_up(to_up, on_up)

        return end

    def cut(s):
        row, col = corners[0, s], corners[1, s]
        block, shift = col // LANES, lax.rem(col, LANES)
        keep = lane >= shift
        rows = pl.ds(row, extent)
        waves = []
        for k in range(2):
            halves = []
            for t in range(2):
                if k == 0:
                    halves.append(jnp.where(keep, field[block, t, rows, :], field[block + 2, t, rows, :]))
                else:
                    halves.append(field[block + 1, t, rows, :])
            lanes = slice(k * LANES, (k + 1) * LANES)
            probe_re, probe_im = turned[s, 0, :, lanes], turned[s, 1, :, lanes]
            waves.append((probe_re * halves[0] - probe_im * halves[1], probe_re * halves[1] + probe_im * halves[0]))
        (re0, im0), (re1, im1) = waves
        even = jnp.concatenate([(re0 + re1).astype(BF16), (im0 + im1).astype(BF16)], 1)
        odd = jnp.concatenate([(re0 - re1).astype(BF16), (im0 - im1).astype(BF16)], 1)
        return even, odd

    def put(s, back):
        keep = lane >= lax.rem(corners[1, s], LANES)
        rows = slice(tile, tile + extent)
        for k in range(2):
            lanes = slice(k * LANES, (k + 1) * LANES)
            probe_re, probe_im = turned[s, 0, :, lanes], turned[s, 1, :, lanes]
            re, im = back[:extent, lanes], back[extent:, lanes]
            for t in range(2):
                if t == 0:
                    term = probe_re * re + probe_im * im
                else:
                    term = probe_re * im - probe_im * re
                if k == 0:
                    zero = jnp.zeros_like(term)
                    patches[3 * s, t, rows] = jnp.where(keep, term, zero)
                    patches[3 * s + 2, t, rows] = jnp.where(keep, zero, term)
                else:
                    patches[3 * s + 1, t, rows] = term

    def matmul(a, b):
        return jnp.dot(a, b, preferred_element_type=F32)

    def patch_of(s):
        return slice(s * extent, (s + 1) * extent)

    def forward(waves):
        by_column = [matmul(jnp.concatenate([wave[q] for wave in waves], 0), table_f[q]).astype(BF16) for q in range(2)]
        operands = [[], []]
        for g in range(len(waves)):
            quarters = [[], []]
            for q in range(2):
                top = by_column[q][g * extent:g * extent + half]
                low = by_column[q][g * extent + half:(g + 1) * extent]
                for p, value in ((0, top + low), (1, top - low)):
                    quarters[p].append(jnp.concatenate([value[:, :half], value[:, half:]], 0))
            for p in range(2):
                operands[p].append(jnp.concatenate(quarters[p], 1))
        return [matmul(table_f[2 + p], jnp.concatenate(operands[p], 1)) for p in range(2)]

    def backward(mixed):
        even, odd = (matmul(jnp.concatenate([m[q] for m in mixed], 0), table_g[q]).astype(BF16) for q in range(2))
        operands = [[], []]
        for g in range(len(mixed)):
            e, o = even[patch_of(g)], odd[patch_of(g)]
            sides = e + o, e - o
            for p in range(2):
                rows = slice(p * half, (p + 1) * half)
                re = jnp.concatenate([side[rows, :half] for side in sides], 1)
                im = jnp.concatenate([side[rows, half:] for side in sides], 1)
                operands[p].append(jnp.concatenate([re, im], 0))
        even, odd = (matmul(table_g[2 + p], jnp.concatenate(operands[p], 1)) for p in range(2))
        backs = []
        for g in range(len(mixed)):
            e, o = even[:, patch_of(g)], odd[:, patch_of(g)]
            top, low = e + o, e - o
            backs.append(jnp.concatenate([top[:half], low[:half], top[half:], low[half:]], 0))
        return backs

    def sweep(kind, slot_energy):
        image = forward([cut(s) for s in range(slots)])
        mixed, squares = [], None
        for s in range(slots):
            parts = [[], []]
            for p in range(2):
                rows = slice(p * half, (p + 1) * half)
                re, im = image[p][:half, patch_of(s)], image[p][half:, patch_of(s)]
                if kind == "first":
                    psi_ref[s, 0, rows] = re
                    psi_ref[s, 1, rows] = im
                    weight = re * re + im * im - measured[s, rows].astype(F32)
                    psi_re, psi_im = re, im
                else:
                    psi_re, psi_im = psi_ref[s, 0, rows], psi_ref[s, 1, rows]
                    weight = psi_re * re + psi_im * im
                    square = weight * weight
                    square = jnp.sum((square[:, :half] + square[:, half:]).reshape(-1, 8, half), 0)
                    squares = square if squares is None else squares + square
                if kind != "last":
                    pair = (psi_re * weight).astype(BF16), (psi_im * weight).astype(BF16)
                    for q in range(2):
                        parts[q].append(jnp.concatenate([x[:, q * half:(q + 1) * half] for x in pair], 1))
            if kind != "last":
                mixed.append([jnp.concatenate(part, 0) for part in parts])
        if kind != "first":
            energy[slot_energy] = squares
        if kind != "last":
            for s, back in enumerate(backward(mixed)):
                put(s, back)

    def gather(start):
        for b in range(4):
            for t in range(2):
                acc = None
                for s in range(slots):
                    row, block = corners[0, s], corners[1, s] // LANES
                    offset = b - block
                    inside = (offset >= 0) & (offset < 3)
                    index = jnp.where(inside, 3 * s + offset, 3 * slots)
                    part = patches[index, t, pl.ds(tile + start - row, size), :]
                    acc = part if acc is None else acc + part
                yield b, t, acc

    def exchange(e, boxes, tiles, sems):
        bottom, inbox_down, side_out, side_in, left_out, left_in = boxes
        own, right, below, corner = tiles
        to_up, on_up = margin_sends(own, right, below, corner, sems, 0)
        to_down = [remote(bottom.at[:, :, r], inbox_down.at[:, :, r], sems, 2 * CHUNKS + c, down) for c, r in enumerate(spans)]
        to_right = [remote(side_out.at[:, :, r], side_in.at[:, :, r], sems, 3 * CHUNKS + c, right_peer) for c, r in enumerate(spans)]
        to_left = [remote(left_out.at[:, :, r], left_in.at[:, :, r], sems, 4 * CHUNKS + c, left) for c, r in enumerate(spans)]

        for c, rows in enumerate(spans):
            for b, t, acc in gather(tile + c * size):
                bottom[b, t, rows] = acc.astype(BF16)

            @when(has_down)
            def _():
                to_down[c].start()

        def send_sideways(c):
            @when(has_right)
            def _():
                side_out[:, :, spans[c]] = total[2:4, :, spans[c]].astype(BF16)
                to_right[c].start()

            @when(has_left)
            def _():
                left_out[:, :, spans[c]] = total[0:2, :, spans[c]].astype(BF16)
                to_left[c].start()

        for c, rows in enumerate(spans):
            for b, t, acc in gather(c * size):
                total[b, t, rows] = acc

            @when(jnp.logical_not(has_up))
            def _():
                send_sideways(c)

        @when(has_up)
        def _():
            for c, rows in enumerate(spans):
                to_down[c].wait_recv()
                total[:, :, rows] += inbox_down[:, :, rows].astype(F32)
                send_sideways(c)

        def scaled(sums, old, rows):
            if e == 0:
                return -2.0 * sums
            return (4.0 * SCALE) * sums + (damping[0] * SCALE) * old[0, :, :, rows]

        for c, rows in enumerate(spans):
            @when(has_left)
            def _():
                to_right[c].wait_recv()
                total[0:2, :, rows] += side_in[:, :, rows].astype(F32)

            value = scaled(total[0:2, :, rows], q, rows)
            q[e, :, :, rows] = value
            own[:, :, rows] = value.astype(BF16)
            field[0:2, :, rows] = own[:, :, rows].astype(F32)

            @when(has_up)
            def _():
                to_up[c].start()

            @when(has_right)
            def _():
                to_left[c].wait_recv()
                value = scaled(total[2:4, :, rows] + left_in[:, :, rows].astype(F32), q_right, rows)
                if e == 0:
                    q_right[e, :, :, rows] = value
                right[:, :, rows] = value.astype(BF16)

                @when(has_up)
                def _():
                    on_up[c].start()

                field[2:4, :, rows] = right[:, :, rows].astype(F32)

        take_below(below, corner, to_up, on_up)

        def end():
            @when(has_down)
            def _():
                for copy in to_down:
                    copy.wait_send()

            @when(has_right)
            def _():
                for copy in to_right:
                    copy.wait_send()

            @when(has_left)
            def _():
                for copy in to_left:
                    copy.wait_send()

            end_up(to_up, on_up)

        return end

    ends = [spread()]
    sweep("first", None)
    ends.append(exchange(0, boxes0, tiles1, (send1, recv1)))
    sweep("middle", 0)
    ends.append(exchange(1, boxes1, tiles2, (send2, recv2)))
    q0, q1 = q[0], q[1]
    rows = [lane_sums(q0 * q0), lane_sums(q1 * q1), lane_sums(energy[0])]
    sweep("last", 1)
    partial = jnp.concatenate(rows + [lane_sums(energy[1]), jnp.zeros((4, LANES), F32)], 0)

    def reduce_over(partial, sums, send, recv, axis, me, n):
        sums[me] = partial
        copies = [
            remote(sums.at[me], sums.at[me], (send, recv), step, {axis: lax.rem(me + step, n)}) for step in range(1, n)
        ]
        for copy in copies:
            copy.start()
        for copy in copies:
            copy.wait()
        return jnp.sum(sums[...], 0)

    partial = reduce_over(partial, sums_y, send_y, recv_y, "ty", ty, n_y)
    partial = reduce_over(partial, sums_x, send_x, recv_x, "tx", tx, n_x)
    dots = jnp.sum(partial, 1, keepdims=True)
    rr, s11, w00, w11 = (dots[k:k + 1] for k in range(4))
    c01 = SCALE * (4.0 * w00 + damping[0] * rr)
    s12 = SCALE * (4.0 * w11 + damping[0] * s11)
    alpha = rr / c01
    rr_next = rr - 2.0 * alpha * c01 + alpha * alpha * s11
    gain = 1.0 + rr_next / rr
    curvature = gain * gain * c01 - 2.0 * gain * alpha * s11 + alpha * alpha * s12
    step_len = rr_next / curvature
    first = (alpha + step_len * gain) * SCALE
    second = step_len * alpha * SCALE
    for h in range(2):
        for t in range(2):
            out_ref[t, :, h * LANES:(h + 1) * LANES] = first * q[0, h, t] - second * q[1, h, t]
    for end in ends:
        end()


def per_device(object_field, probe_field, corners, counts, intensity, damping):
    extent = probe_field.shape[-1]
    tile = object_field.shape[1]
    slots = corners.shape[2]
    n_y, n_x = lax.axis_size("ty"), lax.axis_size("tx")
    places = corners.reshape(slots, 2).T
    measured = intensity.reshape(slots, extent, extent)

    def vmem(shape, dtype):
        return pltpu.VMEM(shape, dtype)

    def sems(n):
        return [pltpu.SemaphoreType.DMA((n,)), pltpu.SemaphoreType.DMA((n,))]

    quarter, whole = (2, 2, tile, LANES), (4, 2, tile, LANES)
    tiles = [vmem(quarter, BF16)] * 4
    boxes = [vmem(whole, BF16)] * 2 + [vmem(quarter, BF16)] * 4
    return pl.pallas_call(
        functools.partial(step_kernel, n_y, n_x),
        out_shape=jax.ShapeDtypeStruct((2, tile, tile), F32),
        in_specs=[SMEM_SPEC] * 3 + [ANY_SPEC] * 5,
        out_specs=pl.BlockSpec(memory_space=pltpu.VMEM),
        scratch_shapes=[
            vmem(probe_field.shape, F32),
            vmem(measured.shape, BF16),
            vmem((4, extent, extent), BF16),
            vmem((4, extent, extent), BF16),
            vmem((slots, 2, extent, extent), F32),
            vmem((slots, 2, extent, extent), F32),
            vmem((4, 2, 2 * tile, LANES), F32),
            vmem((3 * slots + 1, 2, 2 * tile + extent, LANES), F32),
            vmem(whole, F32),
            vmem((2, 8, LANES), F32),
            vmem((2,) + quarter, F32),
            vmem((1,) + quarter, F32),
            tiles, tiles, tiles, boxes, boxes,
            vmem((n_y, 8, LANES), F32),
            vmem((n_x, 8, LANES), F32),
            pltpu.SemaphoreType.DMA((8,)),
        ] + sems(3 * CHUNKS) + sems(5 * CHUNKS) + sems(5 * CHUNKS) + sems(n_y) + sems(n_x),
        compiler_params=pltpu.CompilerParams(collective_id=0, has_side_effects=True, vmem_limit_bytes=58 << 20),
        name="step",
    )(places, counts.reshape(1), damping.reshape(1), object_field, probe_field, measured,
      make_tables(extent, -1.0), make_tables(extent, 1.0))


def solution(mesh):
    in_specs = (
        P(None, "ty", "tx"),
        P(),
        P("ty", "tx", None, None),
        P("ty", "tx"),
        P("ty", "tx", None, None, None),
        P(),
    )
    out_specs = P(None, "ty", "tx")
    return jax.shard_map(
        per_device, mesh=mesh, in_specs=in_specs, out_specs=out_specs, check_vma=False
    )
```

```python
import functools

import jax
import jax.numpy as jnp
import numpy as np
from jax import lax
from jax.experimental import pallas as pl
from jax.experimental.pallas import tpu as pltpu
from jax.sharding import PartitionSpec as P

MESH = pl.DeviceIdType.MESH
LANES = 128
SCALE = 2.0**-24
CHUNKS = 4
F32 = jnp.float32
BF16 = jnp.bfloat16
SMEM_SPEC = pl.BlockSpec(memory_space=pltpu.SMEM)
ANY_SPEC = pl.BlockSpec(memory_space=pl.ANY)


def make_tables(extent, direction_sign):
    indices = np.arange(extent)
    angles = (indices[:, None] * indices[None, :] % extent) * (2.0 * np.pi / extent)
    cosine = np.cos(angles) / extent**0.5
    sines = direction_sign * np.sin(angles) / extent**0.5
    tables = []
    for parity in range(2):
        re, im = cosine[:extent // 2, parity::2], sines[:extent // 2, parity::2]
        if direction_sign > 0:
            re, im = re.T, im.T
        tables.append(np.block([[re, im], [-im, re]]))
    tables = np.stack(tables + [table.T for table in tables])
    return jnp.asarray(tables.astype(np.float32)).astype(BF16)


def lane_sums(values):
    return jnp.sum(values.reshape(-1, LANES), 0, keepdims=True)


def step_kernel(n_y, n_x, corners, count, damping, object_hbm, probe_hbm, measured_hbm, f_hbm, g_hbm, out_ref,
                probe, measured, table_f, table_g, turned, psi_ref, field, patches, total, energy, q, q_right,
                tiles0, tiles1, tiles2, boxes0, boxes1, sums_y, sums_x,
                local_sem, send0, recv0, send1, recv1, send2, recv2, send_y, recv_y, send_x, recv_x):
    slots, extent, tile = turned.shape[0], probe.shape[-1], total.shape[2]
    half = extent // 2
    ty, tx = lax.axis_index("ty"), lax.axis_index("tx")
    has_up, has_down, has_left, has_right = ty > 0, ty < n_y - 1, tx > 0, tx < n_x - 1
    up, down, left, right_peer = {"ty": ty - 1}, {"ty": ty + 1}, {"tx": tx - 1}, {"tx": tx + 1}
    size = tile // CHUNKS
    spans = [pl.ds(c * size, size) for c in range(CHUNKS)]
    lower = [pl.ds(tile + c * size, size) for c in range(CHUNKS)]

    def remote(src, dst, sems, index, peer):
        return pltpu.make_async_remote_copy(
            src_ref=src, dst_ref=dst, send_sem=sems[0].at[index], recv_sem=sems[1].at[index],
            device_id=peer, device_id_type=MESH,
        )

    own0 = tiles0[0]
    fetch = [pltpu.make_async_copy(object_hbm, own0, local_sem.at[0])]
    later = [
        pltpu.make_async_copy(src, dst, local_sem.at[4 + k])
        for k, (src, dst) in enumerate(
            ((probe_hbm, probe), (f_hbm, table_f), (g_hbm, table_g), (measured_hbm, measured))
        )
    ]
    for copy in fetch + later:
        copy.start()
    barrier = pltpu.get_barrier_semaphore()
    for axis, me, n in (("ty", ty, n_y), ("tx", tx, n_x)):
        for step in range(1, n):
            pl.semaphore_signal(barrier, inc=1, device_id={axis: lax.rem(me + step, n)}, device_id_type=MESH)

    def when(*conditions):
        condition = conditions[0]
        for other in conditions[1:]:
            condition = condition & other
        return pl.when(condition)

    lane = lax.broadcasted_iota(jnp.int32, (extent, LANES), 1)
    live = count[0]

    def turn_probe(s):
        shift = lax.rem(corners[1, s], LANES)
        keep = lane >= shift
        for t in range(2):
            near = pltpu.roll(probe[t, :, 0:LANES], shift, 1)
            far = pltpu.roll(probe[t, :, LANES:], shift, 1)
            zero = jnp.zeros_like(near)
            turned[s, t, :, 0:LANES] = jnp.where(s < live, jnp.where(keep, near, far), zero)
            turned[s, t, :, LANES:] = jnp.where(s < live, jnp.where(keep, far, near), zero)

    def margin_sends(own, right, below, corner, sems, base):
        to_up = [remote(own.at[:, :, r], below.at[:, :, r], sems, base + c, up) for c, r in enumerate(spans)]
        on_up = [remote(right.at[:, :, r], corner.at[:, :, r], sems, base + CHUNKS + c, up) for c, r in enumerate(spans)]
        return to_up, on_up

    def widen(block, to_rows, ref, rows):
        for h in range(2):
            for t in range(2):
                source = ref[t, rows, h * LANES:(h + 1) * LANES] if len(ref.shape) == 3 else ref[h, t, rows]
                field[block + h, t, to_rows] = source.astype(F32)

    def take_below(below, corner, to_up, on_up):
        for c in range(CHUNKS):
            @when(has_down)
            def _():
                to_up[c].wait_recv()
                widen(0, lower[c], below, spans[c])

            @when(has_down, has_right)
            def _():
                on_up[c].wait_recv()
                widen(2, lower[c], corner, spans[c])

    def end_up(to_up, on_up):
        @when(has_up)
        def _():
            for copy in to_up:
                copy.wait_send()

        @when(has_up, has_right)
        def _():
            for copy in on_up:
                copy.wait_send()

    def spread():
        own, right, below, corner = tiles0
        sems = (send0, recv0)
        to_up = [remote(object_hbm.at[:, r], below.at[:, r], sems, c, up) for c, r in enumerate(spans)]
        on_up = [remote(right.at[:, r], corner.at[:, r], sems, CHUNKS + c, up) for c, r in enumerate(spans)]
        to_left = [remote(object_hbm.at[:, r], right.at[:, r], sems, 2 * CHUNKS + c, left) for c, r in enumerate(spans)]
        pl.semaphore_wait(barrier, n_y + n_x - 2)
        for c in range(CHUNKS):
            @when(has_left)
            def _():
                to_left[c].start()

            @when(has_up)
            def _():
                to_up[c].start()

        for copy in fetch:
            copy.wait()
        widen(0, pl.ds(0, tile), own, pl.ds(0, tile))
        later[0].wait()

        def turn(s, carry):
            turn_probe(s)
            return carry

        lax.fori_loop(0, slots, turn, 0)
        for copy in later[1:]:
            copy.wait()
        first_index = lax.broadcasted_iota(jnp.int32, (extent, extent), 0)
        second_index = lax.broadcasted_iota(jnp.int32, (extent, extent), 1)
        pick_left = (second_index == 2 * lax.rem(first_index, half) + first_index // half).astype(F32).astype(BF16)
        pick_right = (first_index == 2 * lax.rem(second_index, half) + second_index // half).astype(F32).astype(BF16)

        def reorder(s, carry):
            moved = jnp.dot(measured[s], pick_right, preferred_element_type=F32).astype(BF16)
            measured[s] = jnp.dot(pick_left, moved, preferred_element_type=F32).astype(BF16)
            return carry

        lax.fori_loop(0, slots, reorder, 0)

        @when(jnp.logical_not(has_right))
        def _():
            field[2:4] = jnp.zeros_like(field[2:4])

        @when(jnp.logical_not(has_down))
        def _():
            field[:, :, tile:] = jnp.zeros_like(field[:, :, tile:])

        for c in range(CHUNKS):
            @when(has_right)
            def _():
                to_left[c].wait_recv()

                @when(has_up)
                def _():
                    on_up[c].start()

                widen(2, spans[c], right, spans[c])

        def clear(k, carry):
            for t in range(2):
                patches[k, t, 0:tile] = jnp.zeros((tile, LANES), F32)
                patches[k, t, tile + extent:] = jnp.zeros((tile, LANES), F32)
            return carry

        lax.fori_loop(0, 3 * slots, clear, 0)
        patches[3 * slots] = jnp.zeros(patches.shape[1:], F32)
        take_below(below, corner, to_up, on_up)

        def end():
            @when(has_left)
            def _():
                for copy in to_left:
                    copy.wait_send()

            end_up(to_up, on_up)

        return end

    def cut(s):
        row, col = corners[0, s], corners[1, s]
        block, shift = col // LANES, lax.rem(col, LANES)
        keep = lane >= shift
        rows = pl.ds(row, extent)
        waves = []
        for k in range(2):
            halves = []
            for t in range(2):
                if k == 0:
                    halves.append(jnp.where(keep, field[block, t, rows, :], field[block + 2, t, rows, :]))
                else:
                    halves.append(field[block + 1, t, rows, :])
            lanes = slice(k * LANES, (k + 1) * LANES)
            probe_re, probe_im = turned[s, 0, :, lanes], turned[s, 1, :, lanes]
            waves.append((probe_re * halves[0] - probe_im * halves[1], probe_re * halves[1] + probe_im * halves[0]))
        (re0, im0), (re1, im1) = waves
        even = jnp.concatenate([(re0 + re1).astype(BF16), (im0 + im1).astype(BF16)], 1)
        odd = jnp.concatenate([(re0 - re1).astype(BF16), (im0 - im1).astype(BF16)], 1)
        return even, odd

    def put(s, back):
        keep = lane >= lax.rem(corners[1, s], LANES)
        rows = slice(tile, tile + extent)
        for k in range(2):
            lanes = slice(k * LANES, (k + 1) * LANES)
            probe_re, probe_im = turned[s, 0, :, lanes], turned[s, 1, :, lanes]
            re, im = back[:extent, lanes], back[extent:, lanes]
            for t in range(2):
                if t == 0:
                    term = probe_re * re + probe_im * im
                else:
                    term = probe_re * im - probe_im * re
                if k == 0:
                    zero = jnp.zeros_like(term)
                    patches[3 * s, t, rows] = jnp.where(keep, term, zero)
                    patches[3 * s + 2, t, rows] = jnp.where(keep, zero, term)
                else:
                    patches[3 * s + 1, t, rows] = term

    def matmul(a, b):
        return jnp.dot(a, b, preferred_element_type=F32)

    def patch_of(s):
        return slice(s * extent, (s + 1) * extent)

    def forward(waves):
        by_column = [matmul(jnp.concatenate([wave[q] for wave in waves], 0), table_f[q]).astype(BF16) for q in range(2)]
        operands = [[], []]
        for g in range(len(waves)):
            quarters = [[], []]
            for q in range(2):
                top = by_column[q][g * extent:g * extent + half]
                low = by_column[q][g * extent + half:(g + 1) * extent]
                for p, value in ((0, top + low), (1, top - low)):
                    quarters[p].append(jnp.concatenate([value[:, :half], value[:, half:]], 0))
            for p in range(2):
                operands[p].append(jnp.concatenate(quarters[p], 1))
        return [matmul(table_f[2 + p], jnp.concatenate(operands[p], 1)) for p in range(2)]

    def backward(mixed):
        even, odd = (matmul(jnp.concatenate([m[q] for m in mixed], 0), table_g[q]).astype(BF16) for q in range(2))
        operands = [[], []]
        for g in range(len(mixed)):
            e, o = even[patch_of(g)], odd[patch_of(g)]
            sides = e + o, e - o
            for p in range(2):
                rows = slice(p * half, (p + 1) * half)
                re = jnp.concatenate([side[rows, :half] for side in sides], 1)
                im = jnp.concatenate([side[rows, half:] for side in sides], 1)
                operands[p].append(jnp.concatenate([re, im], 0))
        even, odd = (matmul(table_g[2 + p], jnp.concatenate(operands[p], 1)) for p in range(2))
        backs = []
        for g in range(len(mixed)):
            e, o = even[:, patch_of(g)], odd[:, patch_of(g)]
            top, low = e + o, e - o
            backs.append(jnp.concatenate([top[:half], low[:half], top[half:], low[half:]], 0))
        return backs

    def sweep(kind, slot_energy):
        image = forward([cut(s) for s in range(slots)])
        mixed, squares = [], None
        for s in range(slots):
            parts = [[], []]
            for p in range(2):
                rows = slice(p * half, (p + 1) * half)
                re, im = image[p][:half, patch_of(s)], image[p][half:, patch_of(s)]
                if kind == "first":
                    psi_ref[s, 0, rows] = re
                    psi_ref[s, 1, rows] = im
                    weight = re * re + im * im - measured[s, rows].astype(F32)
                    psi_re, psi_im = re, im
                else:
                    psi_re, psi_im = psi_ref[s, 0, rows], psi_ref[s, 1, rows]
                    weight = psi_re * re + psi_im * im
                    square = weight * weight
                    square = jnp.sum((square[:, :half] + square[:, half:]).reshape(-1, 8, half), 0)
                    squares = square if squares is None else squares + square
                if kind != "last":
                    pair = (psi_re * weight).astype(BF16), (psi_im * weight).astype(BF16)
                    for q in range(2):
                        parts[q].append(jnp.concatenate([x[:, q * half:(q + 1) * half] for x in pair], 1))
            if kind != "last":
                mixed.append([jnp.concatenate(part, 0) for part in parts])
        if kind != "first":
            energy[slot_energy] = squares
        if kind != "last":
            for s, back in enumerate(backward(mixed)):
                put(s, back)

    def gather(start):
        for b in range(4):
            for t in range(2):
                acc = None
                for s in range(slots):
                    row, block = corners[0, s], corners[1, s] // LANES
                    offset = b - block
                    inside = (offset >= 0) & (offset < 3)
                    index = jnp.where(inside, 3 * s + offset, 3 * slots)
                    part = patches[index, t, pl.ds(tile + start - row, size), :]
                    acc = part if acc is None else acc + part
                yield b, t, acc

    def exchange(e, boxes, tiles, sems):
        bottom, inbox_down, side_out, side_in, left_out, left_in = boxes
        own, right, below, corner = tiles
        to_up, on_up = margin_sends(own, right, below, corner, sems, 0)
        to_down = [remote(bottom.at[:, :, r], inbox_down.at[:, :, r], sems, 2 * CHUNKS + c, down) for c, r in enumerate(spans)]
        to_right = [remote(side_out.at[:, :, r], side_in.at[:, :, r], sems, 3 * CHUNKS + c, right_peer) for c, r in enumerate(spans)]
        to_left = [remote(left_out.at[:, :, r], left_in.at[:, :, r], sems, 4 * CHUNKS + c, left) for c, r in enumerate(spans)]

        for c, rows in enumerate(spans):
            for b, t, acc in gather(tile + c * size):
                bottom[b, t, rows] = acc.astype(BF16)

            @when(has_down)
            def _():
                to_down[c].start()

        def send_sideways(c):
            @when(has_right)
            def _():
                side_out[:, :, spans[c]] = total[2:4, :, spans[c]].astype(BF16)
                to_right[c].start()

            @when(has_left)
            def _():
                left_out[:, :, spans[c]] = total[0:2, :, spans[c]].astype(BF16)
                to_left[c].start()

        for c, rows in enumerate(spans):
            for b, t, acc in gather(c * size):
                total[b, t, rows] = acc

            @when(jnp.logical_not(has_up))
            def _():
                send_sideways(c)

        @when(has_up)
        def _():
            for c, rows in enumerate(spans):
                to_down[c].wait_recv()
                total[:, :, rows] += inbox_down[:, :, rows].astype(F32)
                send_sideways(c)

        def scaled(sums, old, rows):
            if e == 0:
                return -2.0 * sums
            return (4.0 * SCALE) * sums + (damping[0] * SCALE) * old[0, :, :, rows]

        for c, rows in enumerate(spans):
            @when(has_left)
            def _():
                to_right[c].wait_recv()
                total[0:2, :, rows] += side_in[:, :, rows].astype(F32)

            value = scaled(total[0:2, :, rows], q, rows)
            q[e, :, :, rows] = value
            own[:, :, rows] = value.astype(BF16)
            field[0:2, :, rows] = own[:, :, rows].astype(F32)

            @when(has_up)
            def _():
                to_up[c].start()

            @when(has_right)
            def _():
                to_left[c].wait_recv()
                value = scaled(total[2:4, :, rows] + left_in[:, :, rows].astype(F32), q_right, rows)
                if e == 0:
                    q_right[e, :, :, rows] = value
                right[:, :, rows] = value.astype(BF16)

                @when(has_up)
                def _():
                    on_up[c].start()

                field[2:4, :, rows] = right[:, :, rows].astype(F32)

        if e == 1:
            q0, q1 = q[0], q[1]
            known.extend([lane_sums(q0 * q0), lane_sums(q1 * q1), lane_sums(energy[0])])
        take_below(below, corner, to_up, on_up)

        def end():
            @when(has_down)
            def _():
                for copy in to_down:
                    copy.wait_send()

            @when(has_right)
            def _():
                for copy in to_right:
                    copy.wait_send()

            @when(has_left)
            def _():
                for copy in to_left:
                    copy.wait_send()

            end_up(to_up, on_up)

        return end

    known = []
    ends = [spread()]
    sweep("first", None)
    ends.append(exchange(0, boxes0, tiles1, (send1, recv1)))
    sweep("middle", 0)
    ends.append(exchange(1, boxes1, tiles2, (send2, recv2)))
    sweep("last", 1)
    partial = jnp.concatenate(known + [lane_sums(energy[1]), jnp.zeros((4, LANES), F32)], 0)

    def reduce_over(partial, sums, send, recv, axis, me, n):
        sums[me] = partial
        copies = [
            remote(sums.at[me], sums.at[me], (send, recv), step, {axis: lax.rem(me + step, n)}) for step in range(1, n)
        ]
        for copy in copies:
            copy.start()
        for copy in copies:
            copy.wait()
        return jnp.sum(sums[...], 0)

    partial = reduce_over(partial, sums_y, send_y, recv_y, "ty", ty, n_y)
    partial = reduce_over(partial, sums_x, send_x, recv_x, "tx", tx, n_x)
    dots = jnp.sum(partial, 1, keepdims=True)
    rr, s11, w00, w11 = (dots[k:k + 1] for k in range(4))
    c01 = SCALE * (4.0 * w00 + damping[0] * rr)
    s12 = SCALE * (4.0 * w11 + damping[0] * s11)
    alpha = rr / c01
    rr_next = rr - 2.0 * alpha * c01 + alpha * alpha * s11
    gain = 1.0 + rr_next / rr
    curvature = gain * gain * c01 - 2.0 * gain * alpha * s11 + alpha * alpha * s12
    step_len = rr_next / curvature
    first = (alpha + step_len * gain) * SCALE
    second = step_len * alpha * SCALE
    for h in range(2):
        for t in range(2):
            out_ref[t, :, h * LANES:(h + 1) * LANES] = first * q[0, h, t] - second * q[1, h, t]
    for end in ends:
        end()


def per_device(object_field, probe_field, corners, counts, intensity, damping):
    extent = probe_field.shape[-1]
    tile = object_field.shape[1]
    slots = corners.shape[2]
    n_y, n_x = lax.axis_size("ty"), lax.axis_size("tx")
    places = corners.reshape(slots, 2).T
    measured = intensity.reshape(slots, extent, extent)

    def vmem(shape, dtype):
        return pltpu.VMEM(shape, dtype)

    def sems(n):
        return [pltpu.SemaphoreType.DMA((n,)), pltpu.SemaphoreType.DMA((n,))]

    quarter, whole = (2, 2, tile, LANES), (4, 2, tile, LANES)
    tiles = [vmem(quarter, BF16)] * 4
    object_tiles = [vmem(object_field.shape, BF16)] * 4
    boxes = [vmem(whole, BF16)] * 2 + [vmem(quarter, BF16)] * 4
    return pl.pallas_call(
        functools.partial(step_kernel, n_y, n_x),
        out_shape=jax.ShapeDtypeStruct((2, tile, tile), F32),
        in_specs=[SMEM_SPEC] * 3 + [ANY_SPEC] * 5,
        out_specs=pl.BlockSpec(memory_space=pltpu.VMEM),
        scratch_shapes=[
            vmem(probe_field.shape, F32),
            vmem(measured.shape, BF16),
            vmem((4, extent, extent), BF16),
            vmem((4, extent, extent), BF16),
            vmem((slots, 2, extent, extent), F32),
            vmem((slots, 2, extent, extent), F32),
            vmem((4, 2, 2 * tile, LANES), F32),
            vmem((3 * slots + 1, 2, 2 * tile + extent, LANES), F32),
            vmem(whole, F32),
            vmem((2, 8, LANES), F32),
            vmem((2,) + quarter, F32),
            vmem((1,) + quarter, F32),
            object_tiles, tiles, tiles, boxes, boxes,
            vmem((n_y, 8, LANES), F32),
            vmem((n_x, 8, LANES), F32),
            pltpu.SemaphoreType.DMA((8,)),
        ] + sems(3 * CHUNKS) + sems(5 * CHUNKS) + sems(5 * CHUNKS) + sems(n_y) + sems(n_x),
        compiler_params=pltpu.CompilerParams(collective_id=0, has_side_effects=True, vmem_limit_bytes=58 << 20),
        name="step",
    )(places, counts.reshape(1), damping.reshape(1), object_field, probe_field, measured,
      make_tables(extent, -1.0), make_tables(extent, 1.0))


def solution(mesh):
    in_specs = (
        P(None, "ty", "tx"),
        P(),
        P("ty", "tx", None, None),
        P("ty", "tx"),
        P("ty", "tx", None, None, None),
        P(),
    )
    out_specs = P(None, "ty", "tx")
    return jax.shard_map(
        per_device, mesh=mesh, in_specs=in_specs, out_specs=out_specs, check_vma=False
    )
```

```python
import functools

import jax
import jax.numpy as jnp
import numpy as np
from jax import lax
from jax.experimental import pallas as pl
from jax.experimental.pallas import tpu as pltpu
from jax.sharding import PartitionSpec as P

MESH = pl.DeviceIdType.MESH
LANES = 128
SCALE = 2.0**-24
CHUNKS = 4
F32 = jnp.float32
BF16 = jnp.bfloat16
SMEM_SPEC = pl.BlockSpec(memory_space=pltpu.SMEM)
ANY_SPEC = pl.BlockSpec(memory_space=pl.ANY)


def make_tables(extent, direction_sign):
    indices = np.arange(extent)
    angles = (indices[:, None] * indices[None, :] % extent) * (2.0 * np.pi / extent)
    cosine = np.cos(angles) / extent**0.5
    sines = direction_sign * np.sin(angles) / extent**0.5
    tables = []
    for parity in range(2):
        re, im = cosine[:extent // 2, parity::2], sines[:extent // 2, parity::2]
        if direction_sign > 0:
            re, im = re.T, im.T
        tables.append(np.block([[re, im], [-im, re]]))
    tables = np.stack(tables + [table.T for table in tables])
    return jnp.asarray(tables.astype(np.float32)).astype(BF16)


def lane_sums(values):
    return jnp.sum(values.reshape(-1, LANES), 0, keepdims=True)


def step_kernel(n_y, n_x, corners, count, damping, object_hbm, probe_hbm, measured_hbm, f_hbm, g_hbm, out_ref,
                probe, measured, table_f, table_g, turned, psi_ref, field, patches, total, energy, q, q_right,
                tiles0, tiles1, tiles2, boxes0, boxes1, sums_y, sums_x,
                local_sem, send0, recv0, send1, recv1, send2, recv2, send_y, recv_y, send_x, recv_x):
    slots, extent, tile = turned.shape[0], probe.shape[-1], total.shape[2]
    half = extent // 2
    ty, tx = lax.axis_index("ty"), lax.axis_index("tx")
    has_up, has_down, has_left, has_right = ty > 0, ty < n_y - 1, tx > 0, tx < n_x - 1
    up, down, left, right_peer = {"ty": ty - 1}, {"ty": ty + 1}, {"tx": tx - 1}, {"tx": tx + 1}
    size = tile // CHUNKS
    spans = [pl.ds(c * size, size) for c in range(CHUNKS)]
    lower = [pl.ds(tile + c * size, size) for c in range(CHUNKS)]

    def remote(src, dst, sems, index, peer):
        return pltpu.make_async_remote_copy(
            src_ref=src, dst_ref=dst, send_sem=sems[0].at[index], recv_sem=sems[1].at[index],
            device_id=peer, device_id_type=MESH,
        )

    own0 = tiles0[0]
    fetch = [pltpu.make_async_copy(object_hbm, own0, local_sem.at[0])]
    later = [
        pltpu.make_async_copy(src, dst, local_sem.at[4 + k])
        for k, (src, dst) in enumerate(
            ((probe_hbm, probe), (f_hbm, table_f), (g_hbm, table_g), (measured_hbm, measured))
        )
    ]
    for copy in fetch + later:
        copy.start()
    barrier = pltpu.get_barrier_semaphore()
    for axis, me, n in (("ty", ty, n_y), ("tx", tx, n_x)):
        for step in range(1, n):
            pl.semaphore_signal(barrier, inc=1, device_id={axis: lax.rem(me + step, n)}, device_id_type=MESH)

    def when(*conditions):
        condition = conditions[0]
        for other in conditions[1:]:
            condition = condition & other
        return pl.when(condition)

    lane = lax.broadcasted_iota(jnp.int32, (extent, LANES), 1)
    live = count[0]

    def turn_probe(s):
        shift = lax.rem(corners[1, s], LANES)
        keep = lane >= shift
        for t in range(2):
            near = pltpu.roll(probe[t, :, 0:LANES], shift, 1)
            far = pltpu.roll(probe[t, :, LANES:], shift, 1)
            zero = jnp.zeros_like(near)
            turned[s, t, :, 0:LANES] = jnp.where(s < live, jnp.where(keep, near, far), zero)
            turned[s, t, :, LANES:] = jnp.where(s < live, jnp.where(keep, far, near), zero)

    def margin_sends(own, right, below, corner, sems, base):
        to_up = [remote(own.at[:, :, r], below.at[:, :, r], sems, base + c, up) for c, r in enumerate(spans)]
        on_up = [remote(right.at[:, :, r], corner.at[:, :, r], sems, base + CHUNKS + c, up) for c, r in enumerate(spans)]
        return to_up, on_up

    def widen(block, to_rows, ref, rows):
        for h in range(2):
            for t in range(2):
                source = ref[t, rows, h * LANES:(h + 1) * LANES] if len(ref.shape) == 3 else ref[h, t, rows]
                field[block + h, t, to_rows] = source.astype(F32)

    def take_below(below, corner, to_up, on_up):
        for c in range(CHUNKS):
            @when(has_down)
            def _():
                to_up[c].wait_recv()
                widen(0, lower[c], below, spans[c])

            @when(has_down, has_right)
            def _():
                on_up[c].wait_recv()
                widen(2, lower[c], corner, spans[c])

    def end_up(to_up, on_up):
        @when(has_up)
        def _():
            for copy in to_up:
                copy.wait_send()

        @when(has_up, has_right)
        def _():
            for copy in on_up:
                copy.wait_send()

    def spread():
        own, right, below, corner = tiles0
        sems = (send0, recv0)
        to_up = [remote(object_hbm.at[:, r], below.at[:, r], sems, c, up) for c, r in enumerate(spans)]
        on_up = [remote(right.at[:, r], corner.at[:, r], sems, CHUNKS + c, up) for c, r in enumerate(spans)]
        to_left = [remote(object_hbm.at[:, r], right.at[:, r], sems, 2 * CHUNKS + c, left) for c, r in enumerate(spans)]
        pl.semaphore_wait(barrier, n_y + n_x - 2)
        for c in range(CHUNKS):
            @when(has_left)
            def _():
                to_left[c].start()

            @when(has_up)
            def _():
                to_up[c].start()

        for copy in fetch:
            copy.wait()
        widen(0, pl.ds(0, tile), own, pl.ds(0, tile))
        later[0].wait()

        def turn(s, carry):
            turn_probe(s)
            return carry

        lax.fori_loop(0, slots, turn, 0)
        for copy in later[1:]:
            copy.wait()
        first_index = lax.broadcasted_iota(jnp.int32, (extent, extent), 0)
        second_index = lax.broadcasted_iota(jnp.int32, (extent, extent), 1)
        pick_left = (second_index == 2 * lax.rem(first_index, half) + first_index // half).astype(F32).astype(BF16)
        pick_right = (first_index == 2 * lax.rem(second_index, half) + second_index // half).astype(F32).astype(BF16)

        def reorder(s, carry):
            moved = jnp.dot(measured[s], pick_right, preferred_element_type=F32).astype(BF16)
            measured[s] = jnp.dot(pick_left, moved, preferred_element_type=F32).astype(BF16)
            return carry

        lax.fori_loop(0, slots, reorder, 0)

        def clear(k, carry):
            for t in range(2):
                patches[k, t, 0:tile] = jnp.zeros((tile, LANES), F32)
                patches[k, t, tile + extent:] = jnp.zeros((tile, LANES), F32)
            return carry

        lax.fori_loop(0, 3 * slots, clear, 0)
        patches[3 * slots] = jnp.zeros(patches.shape[1:], F32)
        @when(jnp.logical_not(has_right))
        def _():
            field[2:4] = jnp.zeros_like(field[2:4])

        @when(jnp.logical_not(has_down))
        def _():
            field[:, :, tile:] = jnp.zeros_like(field[:, :, tile:])

        for c in range(CHUNKS):
            @when(has_right)
            def _():
                to_left[c].wait_recv()

                @when(has_up)
                def _():
                    on_up[c].start()

                widen(2, spans[c], right, spans[c])

        take_below(below, corner, to_up, on_up)

        def end():
            @when(has_left)
            def _():
                for copy in to_left:
                    copy.wait_send()

            end_up(to_up, on_up)

        return end

    def cut(s):
        row, col = corners[0, s], corners[1, s]
        block, shift = col // LANES, lax.rem(col, LANES)
        keep = lane >= shift
        rows = pl.ds(row, extent)
        waves = []
        for k in range(2):
            halves = []
            for t in range(2):
                if k == 0:
                    halves.append(jnp.where(keep, field[block, t, rows, :], field[block + 2, t, rows, :]))
                else:
                    halves.append(field[block + 1, t, rows, :])
            lanes = slice(k * LANES, (k + 1) * LANES)
            probe_re, probe_im = turned[s, 0, :, lanes], turned[s, 1, :, lanes]
            waves.append((probe_re * halves[0] - probe_im * halves[1], probe_re * halves[1] + probe_im * halves[0]))
        (re0, im0), (re1, im1) = waves
        even = jnp.concatenate([(re0 + re1).astype(BF16), (im0 + im1).astype(BF16)], 1)
        odd = jnp.concatenate([(re0 - re1).astype(BF16), (im0 - im1).astype(BF16)], 1)
        return even, odd

    def put(s, back):
        keep = lane >= lax.rem(corners[1, s], LANES)
        rows = slice(tile, tile + extent)
        for k in range(2):
            lanes = slice(k * LANES, (k + 1) * LANES)
            probe_re, probe_im = turned[s, 0, :, lanes], turned[s, 1, :, lanes]
            re, im = back[:extent, lanes], back[extent:, lanes]
            for t in range(2):
                if t == 0:
                    term = probe_re * re + probe_im * im
                else:
                    term = probe_re * im - probe_im * re
                if k == 0:
                    zero = jnp.zeros_like(term)
                    patches[3 * s, t, rows] = jnp.where(keep, term, zero)
                    patches[3 * s + 2, t, rows] = jnp.where(keep, zero, term)
                else:
                    patches[3 * s + 1, t, rows] = term

    def matmul(a, b):
        return jnp.dot(a, b, preferred_element_type=F32)

    def patch_of(s):
        return slice(s * extent, (s + 1) * extent)

    def forward(waves):
        by_column = [matmul(jnp.concatenate([wave[q] for wave in waves], 0), table_f[q]).astype(BF16) for q in range(2)]
        operands = [[], []]
        for g in range(len(waves)):
            quarters = [[], []]
            for q in range(2):
                top = by_column[q][g * extent:g * extent + half]
                low = by_column[q][g * extent + half:(g + 1) * extent]
                for p, value in ((0, top + low), (1, top - low)):
                    quarters[p].append(jnp.concatenate([value[:, :half], value[:, half:]], 0))
            for p in range(2):
                operands[p].append(jnp.concatenate(quarters[p], 1))
        return [matmul(table_f[2 + p], jnp.concatenate(operands[p], 1)) for p in range(2)]

    def backward(mixed):
        even, odd = (matmul(jnp.concatenate([m[q] for m in mixed], 0), table_g[q]).astype(BF16) for q in range(2))
        operands = [[], []]
        for g in range(len(mixed)):
            e, o = even[patch_of(g)], odd[patch_of(g)]
            sides = e + o, e - o
            for p in range(2):
                rows = slice(p * half, (p + 1) * half)
                re = jnp.concatenate([side[rows, :half] for side in sides], 1)
                im = jnp.concatenate([side[rows, half:] for side in sides], 1)
                operands[p].append(jnp.concatenate([re, im], 0))
        even, odd = (matmul(table_g[2 + p], jnp.concatenate(operands[p], 1)) for p in range(2))
        backs = []
        for g in range(len(mixed)):
            e, o = even[:, patch_of(g)], odd[:, patch_of(g)]
            top, low = e + o, e - o
            backs.append(jnp.concatenate([top[:half], low[:half], top[half:], low[half:]], 0))
        return backs

    def sweep(kind, slot_energy):
        image = forward([cut(s) for s in range(slots)])
        mixed, squares = [], None
        for s in range(slots):
            parts = [[], []]
            for p in range(2):
                rows = slice(p * half, (p + 1) * half)
                re, im = image[p][:half, patch_of(s)], image[p][half:, patch_of(s)]
                if kind == "first":
                    psi_ref[s, 0, rows] = re
                    psi_ref[s, 1, rows] = im
                    weight = re * re + im * im - measured[s, rows].astype(F32)
                    psi_re, psi_im = re, im
                else:
                    psi_re, psi_im = psi_ref[s, 0, rows], psi_ref[s, 1, rows]
                    weight = psi_re * re + psi_im * im
                    square = weight * weight
                    square = jnp.sum((square[:, :half] + square[:, half:]).reshape(-1, 8, half), 0)
                    squares = square if squares is None else squares + square
                if kind != "last":
                    pair = (psi_re * weight).astype(BF16), (psi_im * weight).astype(BF16)
                    for q in range(2):
                        parts[q].append(jnp.concatenate([x[:, q * half:(q + 1) * half] for x in pair], 1))
            if kind != "last":
                mixed.append([jnp.concatenate(part, 0) for part in parts])
        if kind != "first":
            energy[slot_energy] = squares
        if kind != "last":
            for s, back in enumerate(backward(mixed)):
                put(s, back)

    def gather(start):
        for b in range(4):
            for t in range(2):
                acc = None
                for s in range(slots):
                    row, block = corners[0, s], corners[1, s] // LANES
                    offset = b - block
                    inside = (offset >= 0) & (offset < 3)
                    index = jnp.where(inside, 3 * s + offset, 3 * slots)
                    part = patches[index, t, pl.ds(tile + start - row, size), :]
                    acc = part if acc is None else acc + part
                yield b, t, acc

    def exchange(e, boxes, tiles, sems):
        bottom, inbox_down, side_out, side_in, left_out, left_in = boxes
        own, right, below, corner = tiles
        to_up, on_up = margin_sends(own, right, below, corner, sems, 0)
        to_down = [remote(bottom.at[:, :, r], inbox_down.at[:, :, r], sems, 2 * CHUNKS + c, down) for c, r in enumerate(spans)]
        to_right = [remote(side_out.at[:, :, r], side_in.at[:, :, r], sems, 3 * CHUNKS + c, right_peer) for c, r in enumerate(spans)]
        to_left = [remote(left_out.at[:, :, r], left_in.at[:, :, r], sems, 4 * CHUNKS + c, left) for c, r in enumerate(spans)]

        for c, rows in enumerate(spans):
            for b, t, acc in gather(tile + c * size):
                bottom[b, t, rows] = acc.astype(BF16)

            @when(has_down)
            def _():
                to_down[c].start()

        def send_sideways(c):
            @when(has_right)
            def _():
                side_out[:, :, spans[c]] = total[2:4, :, spans[c]].astype(BF16)
                to_right[c].start()

            @when(has_left)
            def _():
                left_out[:, :, spans[c]] = total[0:2, :, spans[c]].astype(BF16)
                to_left[c].start()

        for c, rows in enumerate(spans):
            for b, t, acc in gather(c * size):
                total[b, t, rows] = acc

            @when(jnp.logical_not(has_up))
            def _():
                send_sideways(c)

        @when(has_up)
        def _():
            for c, rows in enumerate(spans):
                to_down[c].wait_recv()
                total[:, :, rows] += inbox_down[:, :, rows].astype(F32)
                send_sideways(c)

        def scaled(sums, old, rows):
            if e == 0:
                return -2.0 * sums
            return (4.0 * SCALE) * sums + (damping[0] * SCALE) * old[0, :, :, rows]

        for c, rows in enumerate(spans):
            @when(has_left)
            def _():
                to_right[c].wait_recv()
                total[0:2, :, rows] += side_in[:, :, rows].astype(F32)

            value = scaled(total[0:2, :, rows], q, rows)
            q[e, :, :, rows] = value
            own[:, :, rows] = value.astype(BF16)
            field[0:2, :, rows] = own[:, :, rows].astype(F32)

            @when(has_up)
            def _():
                to_up[c].start()

            @when(has_right)
            def _():
                to_left[c].wait_recv()
                value = scaled(total[2:4, :, rows] + left_in[:, :, rows].astype(F32), q_right, rows)
                if e == 0:
                    q_right[e, :, :, rows] = value
                right[:, :, rows] = value.astype(BF16)

                @when(has_up)
                def _():
                    on_up[c].start()

                field[2:4, :, rows] = right[:, :, rows].astype(F32)

        if e == 1:
            q0, q1 = q[0], q[1]
            known.extend([lane_sums(q0 * q0), lane_sums(q1 * q1), lane_sums(energy[0])])
        take_below(below, corner, to_up, on_up)

        def end():
            @when(has_down)
            def _():
                for copy in to_down:
                    copy.wait_send()

            @when(has_right)
            def _():
                for copy in to_right:
                    copy.wait_send()

            @when(has_left)
            def _():
                for copy in to_left:
                    copy.wait_send()

            end_up(to_up, on_up)

        return end

    known = []
    ends = [spread()]
    sweep("first", None)
    ends.append(exchange(0, boxes0, tiles1, (send1, recv1)))
    sweep("middle", 0)
    ends.append(exchange(1, boxes1, tiles2, (send2, recv2)))
    sweep("last", 1)
    partial = jnp.concatenate(known + [lane_sums(energy[1]), jnp.zeros((4, LANES), F32)], 0)

    def reduce_over(partial, sums, send, recv, axis, me, n):
        sums[me] = partial
        copies = [
            remote(sums.at[me], sums.at[me], (send, recv), step, {axis: lax.rem(me + step, n)}) for step in range(1, n)
        ]
        for copy in copies:
            copy.start()
        for copy in copies:
            copy.wait()
        return jnp.sum(sums[...], 0)

    partial = reduce_over(partial, sums_y, send_y, recv_y, "ty", ty, n_y)
    partial = reduce_over(partial, sums_x, send_x, recv_x, "tx", tx, n_x)
    dots = jnp.sum(partial, 1, keepdims=True)
    rr, s11, w00, w11 = (dots[k:k + 1] for k in range(4))
    c01 = SCALE * (4.0 * w00 + damping[0] * rr)
    s12 = SCALE * (4.0 * w11 + damping[0] * s11)
    alpha = rr / c01
    rr_next = rr - 2.0 * alpha * c01 + alpha * alpha * s11
    gain = 1.0 + rr_next / rr
    curvature = gain * gain * c01 - 2.0 * gain * alpha * s11 + alpha * alpha * s12
    step_len = rr_next / curvature
    first = (alpha + step_len * gain) * SCALE
    second = step_len * alpha * SCALE
    for h in range(2):
        for t in range(2):
            out_ref[t, :, h * LANES:(h + 1) * LANES] = first * q[0, h, t] - second * q[1, h, t]
    for end in ends:
        end()


def per_device(object_field, probe_field, corners, counts, intensity, damping):
    extent = probe_field.shape[-1]
    tile = object_field.shape[1]
    slots = corners.shape[2]
    n_y, n_x = lax.axis_size("ty"), lax.axis_size("tx")
    places = corners.reshape(slots, 2).T
    measured = intensity.reshape(slots, extent, extent)

    def vmem(shape, dtype):
        return pltpu.VMEM(shape, dtype)

    def sems(n):
        return [pltpu.SemaphoreType.DMA((n,)), pltpu.SemaphoreType.DMA((n,))]

    quarter, whole = (2, 2, tile, LANES), (4, 2, tile, LANES)
    tiles = [vmem(quarter, BF16)] * 4
    object_tiles = [vmem(object_field.shape, BF16)] * 4
    boxes = [vmem(whole, BF16)] * 2 + [vmem(quarter, BF16)] * 4
    return pl.pallas_call(
        functools.partial(step_kernel, n_y, n_x),
        out_shape=jax.ShapeDtypeStruct((2, tile, tile), F32),
        in_specs=[SMEM_SPEC] * 3 + [ANY_SPEC] * 5,
        out_specs=pl.BlockSpec(memory_space=pltpu.VMEM),
        scratch_shapes=[
            vmem(probe_field.shape, F32),
            vmem(measured.shape, BF16),
            vmem((4, extent, extent), BF16),
            vmem((4, extent, extent), BF16),
            vmem((slots, 2, extent, extent), F32),
            vmem((slots, 2, extent, extent), F32),
            vmem((4, 2, 2 * tile, LANES), F32),
            vmem((3 * slots + 1, 2, 2 * tile + extent, LANES), F32),
            vmem(whole, F32),
            vmem((2, 8, LANES), F32),
            vmem((2,) + quarter, F32),
            vmem((1,) + quarter, F32),
            object_tiles, tiles, tiles, boxes, boxes,
            vmem((n_y, 8, LANES), F32),
            vmem((n_x, 8, LANES), F32),
            pltpu.SemaphoreType.DMA((8,)),
        ] + sems(3 * CHUNKS) + sems(5 * CHUNKS) + sems(5 * CHUNKS) + sems(n_y) + sems(n_x),
        compiler_params=pltpu.CompilerParams(collective_id=0, has_side_effects=True, vmem_limit_bytes=58 << 20),
        name="step",
    )(places, counts.reshape(1), damping.reshape(1), object_field, probe_field, measured,
      make_tables(extent, -1.0), make_tables(extent, 1.0))


def solution(mesh):
    in_specs = (
        P(None, "ty", "tx"),
        P(),
        P("ty", "tx", None, None),
        P("ty", "tx"),
        P("ty", "tx", None, None, None),
        P(),
    )
    out_specs = P(None, "ty", "tx")
    return jax.shard_map(
        per_device, mesh=mesh, in_specs=in_specs, out_specs=out_specs, check_vma=False
    )
```
